32 devices in a mesh: gx: 8 (over z, x), gy: 4 (over y, core).
Axes of the slice: x: 2, y: 2, z: 4, core: 2. Of those that a mesh axis runs over, the one named last changes fastest.
Arguments:
- e_field: float32 [3, 128, 128, 256], P(None, 'gx', 'gy'), may hold values from -6 to 6
- h_field: float32 [3, 128, 128, 256], P(None, 'gx', 'gy'), may hold values from -6 to 6
- material: int32 [128, 128, 256], P('gx', 'gy'), may hold values from 0 to 7
- eps_table: float32 [8], replicated, may hold values from 1 to 12
- forward_dft: bfloat16 [4, 2, 3, 128, 128, 256], P(None, None, None, 'gx', 'gy'), may hold values from -6 to 6
- phase_step: float32 [4], replicated, may hold values from 0.3 to 2.8
- interp_kernels: float32 [4, 1024, 128], replicated, may hold values from -0.1875 to 0.1875
- kernel_id: int32 [64, 64], P('gx', 'gy'), may hold values from 0 to 3
- owner_map: int32 [64, 64], P('gx', 'gy'), may hold values from 0 to 31, as said below
- slot_map: int32 [64, 64], P('gx', 'gy'), may hold values from 0 to 63
Outputs:
- e_out: float32 [3, 128, 128, 256], P(None, 'gx', 'gy')
- h_out: float32 [3, 128, 128, 256], P(None, 'gx', 'gy')
- design_grad: float32 [2048, 128], P(('gx', 'gy'))
The draws below stay inside these ranges and needn't reach their ends.
Inputs may be any that keep to these rules, and one draw needn't show every extreme that they name: `owner_map`: the tiles of one device name no owner more than 8 times; in every draw one owner is named exactly 8 times by the tiles of every device.
All inputs are finite; a program needn't handle non-finite values.
Results may differ from the reference program's by a relative error of at most 0.0003.
Values sent between devices are 32-bit elements; how exact they have to be, the bound alone decides.
A program may use at most 64 MiB of HBM per device.

```python
import math
import jax
import jax.numpy as jnp
from jax import lax

CX = 16
CY = 32
NZ = 256
STEPS = 4
WAVES = 4
MATS = 8
KERNELS = 4
VOX = 128
SLOTS = 64
NX = 128
NY = 128
OWNERS = 32
TILES_DEV = 128
TILE_CELLS = 1024
CAP = 8


def draw_owner_map(key, part):
    grid_x = NX // CX
    grid_y = NY // CY
    common = jax.random.randint(jax.random.fold_in(key, 11), (), 0, OWNERS).astype(jnp.int32)

    def one_device(device):
        subkey = jax.random.fold_in(key, 1000 + device)
        order = jax.random.permutation(jax.random.fold_in(subkey, 1), TILES_DEV)
        pool = jax.random.permutation(jax.random.fold_in(subkey, 2), (OWNERS - 1) * CAP)[:TILES_DEV - CAP] // CAP
        others = (common + 1 + pool.astype(jnp.int32)) % OWNERS
        assign = jnp.concatenate([jnp.zeros((CAP,), jnp.int32) + common, others.astype(jnp.int32)])
        return jnp.zeros((TILES_DEV,), jnp.int32).at[order].set(assign)
    table = jax.vmap(one_device)(jnp.arange(OWNERS, dtype=jnp.int32))
    table = table.reshape(grid_x, grid_y, CX // 2, CY // 2).transpose(0, 2, 1, 3)
    return table.reshape(NX // 2, NY // 2)


def with_ends(array, key, low, top_value):
    longest = array.shape.index(max(array.shape))
    spots = []
    for shift in (0, 1):
        where = [jax.random.randint(jax.random.fold_in(key, axis), (), 0, length) for axis, length in enumerate(array.shape)]
        where[longest] = (where[longest] + shift) % array.shape[longest]
        spots.append(tuple(where))
    return array.at[spots[0]].set(low).at[spots[1]].set(top_value)


def block_levels(rng, shape, cuts, low, largest):
    def one(dim, parts):
        heights = jax.random.uniform(jax.random.fold_in(jax.random.fold_in(rng, 6), dim), (parts,), jnp.float32, low / len(cuts), largest / len(cuts))
        return jnp.repeat(jnp.exp(heights), shape[dim] // parts).reshape((-1,) + (1,) * (len(shape) - dim - 1))

    loudness = one(*cuts[0])
    for cut in cuts[1:]:
        loudness = loudness * one(*cut)
    return loudness


def normal_values(rng, extent, width, bound, split=(), kind=jnp.bfloat16):
    values = jax.random.normal(rng, extent, jnp.float32) * width
    if len(split) > 0:
        values = block_levels(rng, extent, split, -0.22, 0.18) * values
    return jnp.clip(values, min=-bound, max=bound).astype(kind)


def setup_inputs(seed: int = 0) -> dict:
    arg_keys = jax.random.split(jax.random.key(seed), 11)
    e_field = normal_values(arg_keys[0], (3, NX, NY, NZ), 1.0, 6.0, ((1, 8), (2, 4)), jnp.float32)
    h_field = normal_values(arg_keys[1], (3, NX, NY, NZ), 1.0, 6.0, ((1, 8), (2, 4)), jnp.float32)
    material = with_ends(jax.random.randint(arg_keys[2], (NX, NY, NZ), 0, MATS), jax.random.fold_in(arg_keys[2], 1), 0, MATS - 1).astype(jnp.int32)
    eps_table = jnp.clip(jnp.exp(jax.random.uniform(arg_keys[3], (MATS,), jnp.float32, math.log(1.0), math.log(12.0))), 1.0, 12.0)
    forward_dft = normal_values(arg_keys[4], (WAVES, 2, 3, NX, NY, NZ), 1.0, 6.0, ((3, 8), (4, 4)))
    phase_step = jnp.clip(jax.random.uniform(arg_keys[5], (WAVES,), jnp.float32, 0.3, 2.8), 0.3, 2.8)
    interp_kernels = normal_values(arg_keys[6], (KERNELS, TILE_CELLS, VOX), TILE_CELLS ** -0.5, 0.1875, (), jnp.float32)
    kernel_id = with_ends(jax.random.randint(arg_keys[7], (NX // 2, NY // 2), 0, KERNELS), jax.random.fold_in(arg_keys[7], 1), 0, KERNELS - 1).astype(jnp.int32)
    owner_map = draw_owner_map(jax.random.fold_in(arg_keys[10], 71), 0)
    slot_map = with_ends(jax.random.randint(arg_keys[9], (NX // 2, NY // 2), 0, SLOTS), jax.random.fold_in(arg_keys[9], 1), 0, SLOTS - 1).astype(jnp.int32)
    return dict(e_field=e_field, h_field=h_field, material=material, eps_table=eps_table, forward_dft=forward_dft, phase_step=phase_step, interp_kernels=interp_kernels, kernel_id=kernel_id, owner_map=owner_map, slot_map=slot_map)


COURANT = 0.5


def ahead_diff(field, axis):
    widths = [(0, 0), (0, 0), (0, 0)]
    widths[axis] = (0, 1)
    padded = jnp.pad(field, widths)
    return lax.slice_in_dim(padded, 1, field.shape[axis] + 1, axis=axis) - field


def behind_diff(field, axis):
    widths = [(0, 0), (0, 0), (0, 0)]
    widths[axis] = (1, 0)
    padded = jnp.pad(field, widths)
    return field - lax.slice_in_dim(padded, 0, field.shape[axis], axis=axis)


def reference(e_field, h_field, material, eps_table, forward_dft, phase_step, interp_kernels, kernel_id, owner_map, slot_map):
    scale = COURANT / eps_table[material]
    elec_x, elec_y, elec_z = e_field[0], e_field[1], e_field[2]
    magn_x, magn_y, magn_z = h_field[0], h_field[1], h_field[2]
    sens = jnp.zeros(elec_x.shape, jnp.float32)
    for step_index in range(STEPS):
        magn_x = magn_x - COURANT * (ahead_diff(elec_z, 1) - ahead_diff(elec_y, 2))
        magn_y = magn_y - COURANT * (ahead_diff(elec_x, 2) - ahead_diff(elec_z, 0))
        magn_z = magn_z - COURANT * (ahead_diff(elec_y, 0) - ahead_diff(elec_x, 1))
        elec_x = elec_x + scale * (behind_diff(magn_z, 1) - behind_diff(magn_y, 2))
        elec_y = elec_y + scale * (behind_diff(magn_x, 2) - behind_diff(magn_z, 0))
        elec_z = elec_z + scale * (behind_diff(magn_y, 0) - behind_diff(magn_x, 1))
        moment = float(step_index + 1)
        cosines = jnp.cos(phase_step * moment)
        sine_terms = jnp.sin(phase_step * moment)
        elec = (elec_x, elec_y, elec_z)
        for comp in range(3):
            weight = jnp.zeros(elec_x.shape, jnp.float32)
            for wave in range(WAVES):
                weight = weight + forward_dft[wave, 0, comp].astype(jnp.float32) * cosines[wave] - forward_dft[wave, 1, comp].astype(jnp.float32) * sine_terms[wave]
            sens = sens + elec[comp] * weight
    sens = sens / float(WAVES * STEPS)
    tile_rows = sens.reshape(NX // 2, 2, NY // 2, 2, NZ).transpose(0, 2, 1, 3, 4).reshape(-1, 4 * NZ)
    all_kernels = jnp.einsum('tc,kcv->tkv', tile_rows, interp_kernels, precision=lax.Precision.HIGHEST)
    selector = (kernel_id.reshape(-1)[:, None] == jnp.arange(KERNELS, dtype=jnp.int32)[None, :]).astype(jnp.float32)
    restricted = jnp.sum(all_kernels * selector[:, :, None], axis=1)
    target = owner_map.reshape(-1) * SLOTS + slot_map.reshape(-1)
    design_grad = jax.ops.segment_sum(restricted, target, num_segments=OWNERS * SLOTS)
    e_out = jnp.stack([elec_x, elec_y, elec_z])
    h_out = jnp.stack([magn_x, magn_y, magn_z])
    return (e_out, h_out, design_grad)
```

```python
import functools

import jax
import jax.numpy as jnp
from jax import lax
from jax.experimental import pallas as pl
from jax.experimental.pallas import tpu as pltpu
from jax.sharding import PartitionSpec as P

STEPS = 4
SLOTS = 64
COURANT = 0.5
UNROLL = 4

F32 = jnp.float32
BF16 = jnp.bfloat16
MESH = pl.DeviceIdType.MESH


def split2(value):
    high = value.astype(BF16)
    return high, (value - high.astype(F32)).astype(BF16)


def dot(lhs, rhs):
    return jnp.dot(lhs, rhs, preferred_element_type=F32)


def dot_rows(lhs, rhs):
    return lax.dot_general(lhs, rhs, (((0,), (0,)), ((), ())), preferred_element_type=F32)


def iota(shape, dim):
    return lax.broadcasted_iota(jnp.int32, shape, dim)


def as_row(values):
    rows, lanes = values.shape
    size = rows * lanes
    pick = (iota((rows, size), 1) // lanes == iota((rows, size), 0)).astype(BF16)
    spread = dot_rows(values.astype(F32).astype(BF16), pick)
    keep = iota((lanes, size), 0) == lax.rem(iota((lanes, size), 1), lanes)
    return jnp.sum(jnp.where(keep, spread, 0.0), axis=0, keepdims=True)


def kernel(
    size_x,
    size_y,
    capacity,
    eps_ref,
    phase_ref,
    e_in,
    h_in,
    mat_in,
    dft_in,
    kern_in,
    kid_in,
    owner_in,
    slot_in,
    last_elec,
    magn,
    got,
    elec_steps,
    mat,
    scale,
    dft,
    kern,
    kern_high,
    kern_low,
    kid,
    owner,
    slot,
    coefs,
    weights,
    sens,
    halo_ex,
    halo_hx,
    halo_ey,
    halo_hy,
    pack_hx,
    pack_ey,
    pack_hy,
    pack_corner,
    halo_corner,
    put,
    in_sem,
    send_sem,
    recv_sem,
    round_sem,
    a2a_sem,
):
    count = size_x * size_y
    cells_x, cells_y, depth = mat.shape
    waves = dft.shape[0]
    tile_x, tile_y = kid.shape
    tiles = tile_x * tile_y
    kernels, tile_cells, voxels = kern.shape
    gx = lax.axis_index("gx")
    gy = lax.axis_index("gy")
    me = gx * size_y + gy

    elec = [elec_steps.at[step] for step in range(STEPS)] + [last_elec]

    loads = [
        pltpu.make_async_copy(source, target, in_sem.at[place])
        for place, (source, target) in enumerate(
            [
                (e_in, elec[0]),
                (h_in, magn),
                (mat_in, mat),
                (kid_in, kid),
                (owner_in, owner),
                (slot_in, slot),
                (kern_in, kern),
                (dft_in, dft),
            ]
        )
    ]
    for load in loads:
        load.start()

    first_x, last_x = gx > 0, gx < size_x - 1
    first_y, last_y = gy > 0, gy < size_y - 1
    partners = [
        (first_x, -1, 0),
        (last_x, 1, 0),
        (first_y, 0, -1),
        (last_y, 0, 1),
        (last_x & first_y, 1, -1),
        (first_x & last_y, -1, 1),
    ]
    def how_many(conditions):
        return sum(one.astype(jnp.int32) for one in conditions)

    barrier = pltpu.get_barrier_semaphore()
    for there, dx, dy in partners:

        @pl.when(there)
        def _():
            pl.semaphore_signal(
                barrier, inc=1, device_id=(gx + dx, gy + dy), device_id_type=MESH
            )

    def wait_partners():
        pl.semaphore_wait(barrier, how_many(there for there, _, _ in partners))

    rounds = []
    for axis, size in ((1, size_y), (0, size_x)):
        reach = 1
        while reach < size:
            rounds.append((axis, size, reach))
            reach *= 2

    def run_round(index):
        if index >= len(rounds):
            return
        axis, size, reach = rounds[index]
        place = (gx, gy)[axis]
        sides = ((place >= reach, -reach), (place < size - reach, reach))
        for there, shift in sides:

            @pl.when(there)
            def _():
                peer = (gx + shift, gy) if axis == 0 else (gx, gy + shift)
                pl.semaphore_signal(
                    round_sem.at[index], inc=1, device_id=peer, device_id_type=MESH
                )

    def end_round(index):
        if index >= len(rounds):
            return
        axis, size, reach = rounds[index]
        place = (gx, gy)[axis]
        peers = how_many((place >= reach, place < size - reach))
        pl.semaphore_wait(round_sem.at[index], peers)

    row_y = iota((cells_y, depth), 0)
    col_z = iota((cells_y, depth), 1)

    def y_up(v):
        return jnp.where(row_y == cells_y - 1, 0.0, pltpu.roll(v, cells_y - 1, 0))

    def z_up(v):
        return jnp.where(col_z == depth - 1, 0.0, pltpu.roll(v, depth - 1, 1))

    def y_down(v):
        return jnp.where(row_y == 0, 0.0, pltpu.roll(v, 1, 0))

    def z_down(v):
        return jnp.where(col_z == 0, 0.0, pltpu.roll(v, 1, 1))

    def h_plane(step, x, last):
        elec_now = elec[step]
        ex, ey, ez = elec_now[0, x], elec_now[1, x], elec_now[2, x]
        dx_ey = -ey if last else elec_now[1, x + 1] - ey
        dx_ez = -ez if last else elec_now[2, x + 1] - ez
        magn[0, x] = magn[0, x] - COURANT * ((y_up(ez) - ez) - (z_up(ey) - ey))
        magn[1, x] = magn[1, x] - COURANT * ((z_up(ex) - ex) - dx_ez)
        magn[2, x] = magn[2, x] - COURANT * (dx_ey - (y_up(ex) - ex))

    def e_plane(step, x, first):
        elec_now, elec_new = elec[step], elec[step + 1]
        hx, hy, hz = magn[0, x], magn[1, x], magn[2, x]
        dx_hy = hy if first else hy - magn[1, x - 1]
        dx_hz = hz if first else hz - magn[2, x - 1]
        factor = scale[x]
        elec_new[0, x] = elec_now[0, x] + factor * ((hz - y_down(hz)) - (hy - z_down(hy)))
        elec_new[1, x] = elec_now[1, x] + factor * ((hx - z_down(hx)) - dx_hz)
        elec_new[2, x] = elec_now[2, x] + factor * (dx_hy - (hx - y_down(hx)))

    def loop(low, high, body):
        def run(x, carry):
            body(x)
            return carry

        lax.fori_loop(low, high, run, 0)

    def h_interior(step):
        loop(0, cells_x - 1, lambda x: h_plane(step, x, False))

    def e_interior(step):
        e_plane(step, 0, True)
        loop(1, cells_x, lambda x: e_plane(step, x, False))

    def copy(kind, step, source, target, there, back, dx, dy):
        one = pltpu.make_async_remote_copy(
            src_ref=source,
            dst_ref=target,
            send_sem=send_sem.at[kind, step],
            recv_sem=recv_sem.at[kind, step],
            device_id=(gx + dx, gy + dy),
            device_id_type=MESH,
        )
        return there, back, one

    end_x, end_y = cells_x - 1, cells_y - 1
    top, bottom = pl.ds(0, 1), pl.ds(end_y, 1)
    sent = []

    def start(kind, step, *rest):
        there, _, one = copy(kind, step, *rest)
        sent.append((there, one))

        @pl.when(there)
        def _():
            one.start()

    def plans(step):
        corner = pack_corner.at[step]
        return {
            0: (pack_ey.at[step, 0, end_x], halo_corner.at[step, 0], last_x & first_y, first_x & last_y, 1, -1),
            1: (corner, halo_corner.at[step, 1], first_x & last_y, last_x & first_y, -1, 1),
            2: (elec[step].at[pl.ds(1, 2), 0], halo_ex.at[step], first_x, last_x, -1, 0),
            3: (pack_hx.at[step], halo_hx.at[step], last_x, first_x, 1, 0),
            4: (pack_ey.at[step], halo_ey.at[step], first_y, last_y, 0, -1),
            5: (pack_hy.at[step], halo_hy.at[step], last_y, first_y, 0, 1),
        }

    def begin(step, kind):
        start(kind, step, *plans(step)[kind])

    def arrive(step, kind):
        _, _, one = copy(kind, step, *plans(step)[kind])
        one.wait_recv()

    def send_elec(step):
        field = elec[step]
        pack_ey[step, 0] = field[0, :, top, :]
        pack_ey[step, 1] = field[2, :, top, :]
        pack_corner[step] = field[1, 0, bottom, :]
        begin(step, 0)
        begin(step, 1)
        begin(step, 2)
        begin(step, 4)

    def send_magn_x(step):
        h_plane(step, end_x, True)
        pack_hx[step, 0] = magn[1, end_x]
        pack_hx[step, 1] = magn[2, end_x]
        begin(step, 3)

    def send_magn_y(step):
        pack_hy[step, 0] = magn[0, :, bottom, :]
        pack_hy[step, 1] = magn[2, :, bottom, :]
        begin(step, 5)

    def receive(step):
        now, new = elec[step], elec[step + 1]
        col = iota((cells_x, 1, depth), 2)

        @pl.when(last_y)
        def _():
            arrive(step, 4)
            d_hz = COURANT * halo_ey[step, 0]
            d_hx = -COURANT * halo_ey[step, 1]
            magn[0, :, bottom, :] = magn[0, :, bottom, :] + d_hx
            magn[2, :, bottom, :] = magn[2, :, bottom, :] + d_hz
            factor = scale[:, bottom, :]
            before = jnp.concatenate([jnp.zeros_like(d_hz[:1]), d_hz[:-1]], axis=0)
            z_before = jnp.where(col == 0, 0.0, pltpu.roll(d_hx, 1, 2))
            new[0, :, bottom, :] = new[0, :, bottom, :] + factor * d_hz
            new[1, :, bottom, :] = new[1, :, bottom, :] + factor * (
                (d_hx - z_before) - (d_hz - before)
            )
            new[2, :, bottom, :] = new[2, :, bottom, :] - factor * d_hx

        @pl.when(first_y)
        def _():
            arrive(step, 5)
            hx = halo_hy[step, 0] - COURANT * now[2, :, top, :]
            hz = halo_hy[step, 1] + COURANT * now[0, :, top, :]
            factor = scale[:, top, :]
            new[0, :, top, :] = new[0, :, top, :] - factor * hz
            new[2, :, top, :] = new[2, :, top, :] + factor * hx

        @pl.when(first_y & last_x)
        def _():
            arrive(step, 1)
            new[0, end_x, top, :] = new[0, end_x, top, :] + scale[end_x, top, :] * (
                COURANT * halo_corner[step, 1]
            )

        @pl.when(last_x)
        def _():
            arrive(step, 2)
            d_hy = COURANT * halo_ex[step, 1]
            d_hz = -COURANT * halo_ex[step, 0]
            magn[1, end_x] = magn[1, end_x] + d_hy
            magn[2, end_x] = magn[2, end_x] + d_hz
            factor = scale[end_x]
            new[0, end_x] = new[0, end_x] + factor * (
                (d_hz - y_down(d_hz)) - (d_hy - z_down(d_hy))
            )
            new[1, end_x] = new[1, end_x] - factor * d_hz
            new[2, end_x] = new[2, end_x] + factor * d_hy

        @pl.when(first_x & last_y)
        def _():
            arrive(step, 0)
            new[1, 0, bottom, :] = new[1, 0, bottom, :] + scale[0, bottom, :] * (
                COURANT * halo_corner[step, 0]
            )

        @pl.when(first_x)
        def _():
            arrive(step, 3)
            hy = halo_hx[step, 0] + COURANT * now[2, 0]
            hz = halo_hx[step, 1] - COURANT * now[1, 0]
            factor = scale[0]
            new[1, 0] = new[1, 0] + factor * hz
            new[2, 0] = new[2, 0] - factor * hy

    def wait_sent():
        for there, one in sent:

            @pl.when(there)
            def _():
                one.wait_send()

    def make_scale():
        def plane(x):
            kind = mat[x]
            eps = jnp.full(kind.shape, eps_ref[0], F32)
            for index in range(1, eps_ref.shape[0]):
                eps = jnp.where(kind == index, eps_ref[index], eps)
            scale[x] = COURANT / eps

        loop(0, cells_x, plane)

    def make_coefs():
        width = 2 * waves * cells_y
        column = iota((8, width), 1)
        wave = column // (2 * cells_y)
        phase = jnp.full((8, width), phase_ref[0], F32)
        for index in range(1, waves):
            phase = jnp.where(wave == index, phase_ref[index], phase)
        angle = phase * (iota((8, width), 0) + 1).astype(F32)
        imaginary = lax.rem(column // cells_y, 2) == 1
        values = jnp.where(imaginary, -jnp.sin(angle), jnp.cos(angle)) / float(waves * STEPS)
        own = iota((cells_y, width), 0) == lax.rem(iota((cells_y, width), 1), cells_y)
        table = jnp.concatenate(
            [jnp.where(own, values[step : step + 1], 0.0) for step in range(STEPS)], axis=0
        )
        coefs[...] = jnp.concatenate(split2(table), axis=0)

    def make_weights(low, high):
        half = STEPS * cells_y

        def plane(index):
            comp, x = lax.rem(index, 3), index // 3
            block = dft[:, :, comp, x].reshape(2 * waves * cells_y, depth)
            both = dot(coefs[...], block)
            weights[:, comp, x] = (both[:half] + both[half:]).reshape(STEPS, cells_y, depth)

        def several(index):
            for extra in range(UNROLL):
                plane(index * UNROLL + extra)

        loop(low, high, several)

    def add_sens(low, high):
        def plane(x):
            total = None
            for step in range(low, high):
                for comp in range(3):
                    term = elec[step + 1][comp, x] * weights[step, comp, x]
                    total = term if total is None else total + term
            for block in range(depth // 128):
                lanes = total[:, block * 128 : (block + 1) * 128]
                sens[block, x] = lanes if low == 0 else sens[block, x] + lanes

        loop(0, cells_x, plane)

    def as_column(values):
        pick = (iota((tiles, tile_x), 0) // tile_y == iota((tiles, tile_x), 1)).astype(BF16)
        spread = dot(pick, values.astype(F32).astype(BF16))
        keep = iota((tiles, tile_y), 1) == lax.rem(iota((tiles, tile_y), 0), tile_y)
        return jnp.sum(jnp.where(keep, spread, 0.0), axis=1, keepdims=True)

    def positions():
        own_row = as_row(owner[...])
        own_column = as_column(owner[...])
        earlier = (own_column == own_row) & (iota((tiles, tiles), 0) < iota((tiles, tiles), 1))
        rank = jnp.sum(jnp.where(earlier, 1.0, 0.0), axis=0, keepdims=True)
        return own_row, own_column, rank

    def label_slots():
        own_row, _, rank = positions()
        mine = (iota((count, tiles), 0).astype(F32) == own_row).astype(BF16)
        place = (iota((128, tiles), 0).astype(F32) == rank).astype(F32)
        labels = (place * (as_row(slot[...]) + 1.0)).astype(BF16)
        table = (
            lax.dot_general(mine, labels, (((1,), (1,)), ((), ())), preferred_element_type=F32)
            - 1.0
        )
        put[:, pl.ds(capacity, 1), :] = table.reshape(count, 1, 128)

    def wait_all(buffer, place):
        part = buffer.at[pl.ds(0, count - 1)]
        pltpu.make_async_copy(part, part, a2a_sem.at[place]).wait()

    def make_kernels():
        for index in range(kernels):
            high, low = split2(kern[index])
            kern_high[:, index * voxels : (index + 1) * voxels] = high
            kern_low[:, index * voxels : (index + 1) * voxels] = low

    units = 3 * cells_x // UNROLL

    def share(part):
        make_weights(units * part // STEPS, units * (part + 1) // STEPS)

    loads[0].wait()
    wait_partners()
    for step in range(STEPS):
        send_elec(step)
        if step == 0:
            loads[1].wait()
        send_magn_x(step)
        h_interior(step)
        send_magn_y(step)
        run_round(2 * step)
        if step == 0:
            loads[2].wait()
            make_scale()
            make_coefs()
        e_interior(step)
        if step == 0:
            loads[7].wait()
        end_round(2 * step)
        run_round(2 * step + 1)
        share(step)
        if step == 1:
            for place in (3, 4, 5):
                loads[place].wait()
            label_slots()
        if step == STEPS - 1:
            loads[6].wait()
            make_kernels()
            add_sens(0, STEPS - 1)
        receive(step)
        end_round(2 * step + 1)
    for index in range(2 * STEPS, len(rounds)):
        run_round(index)
        end_round(index)
    add_sens(STEPS - 1, STEPS)

    total = jnp.zeros((tiles, kernels * voxels), F32)
    for a in range(2):
        for b in range(2):
            part = [
                sens[block, pl.ds(a, cells_x // 2, 2), pl.ds(b, cells_y // 2, 2), :]
                for block in range(depth // 128)
            ]
            part = jnp.concatenate([lanes.reshape(tiles, 128) for lanes in part], axis=1)
            high, low = split2(part)
            rows = slice((2 * a + b) * depth, (2 * a + b + 1) * depth)
            big, small = kern_high[rows, :], kern_low[rows, :]
            total = total + dot(high, big) + (dot(low, big) + dot(high, small))
    kinds = as_column(kid[...])
    restricted = jnp.zeros((tiles, voxels), F32)
    for index in range(kernels):
        restricted = restricted + jnp.where(
            kinds == float(index), total[:, index * voxels : (index + 1) * voxels], 0.0
        )

    own_row, _, rank = positions()
    position = own_row * float(capacity) + rank
    placement = (iota((count * capacity, tiles), 0).astype(F32) == position).astype(BF16)
    high, low = split2(restricted)
    put[:, pl.ds(0, capacity), :] = (dot(placement, high) + dot(placement, low)).reshape(
        count, capacity, voxels
    )
    got[me] = put[me]

    def push(step, carry):
        peer = lax.rem(me + step, count)
        pltpu.make_async_remote_copy(
            src_ref=put.at[peer],
            dst_ref=got.at[me],
            send_sem=a2a_sem.at[0],
            recv_sem=a2a_sem.at[1],
            device_id=(peer // size_y, lax.rem(peer, size_y)),
            device_id_type=MESH,
        ).start()
        return carry

    lax.fori_loop(1, count, push, 0)
    wait_sent()
    wait_all(got, 1)
    wait_all(put, 0)


def finish(capacity, elec, magn, got, e_out, h_out, grad_ref, sems):
    stores = [
        pltpu.make_async_copy(elec, e_out, sems.at[0]),
        pltpu.make_async_copy(magn, h_out, sems.at[1]),
    ]
    for store in stores:
        store.start()
    count, _, voxels = got.shape
    received = got[:, pl.ds(capacity, 1), :].reshape(count, 128)[:, :capacity]
    gather = (
        iota((SLOTS, count * capacity), 0).astype(F32) == as_row(received)
    ).astype(BF16)
    high, low = split2(got[:, pl.ds(0, capacity), :].reshape(count * capacity, voxels))
    grad_ref[...] = dot(gather, high) + dot(gather, low)
    for store in stores:
        store.wait()


def per_device(
    size_x,
    size_y,
    e_field,
    h_field,
    material,
    eps_table,
    forward_dft,
    phase_step,
    interp_kernels,
    kernel_id,
    owner_map,
    slot_map,
):
    count = size_x * size_y
    cells_x, cells_y, depth = material.shape
    kernels, tile_cells, voxels = interp_kernels.shape
    tiles = cells_x * cells_y // 4
    capacity = max(2, (2 * tiles + count - 1) // count)
    field = jax.ShapeDtypeStruct(e_field.shape, F32)
    anywhere = pl.BlockSpec(memory_space=pltpu.HBM)
    here = pl.BlockSpec(memory_space=pltpu.VMEM)
    state = pl.pallas_call(
        functools.partial(kernel, size_x, size_y, capacity),
        out_shape=(
            pltpu.VMEM(e_field.shape, F32),
            pltpu.VMEM(h_field.shape, F32),
            pltpu.VMEM((count, capacity + 1, voxels), F32),
        ),
        in_specs=[pl.BlockSpec(memory_space=pltpu.SMEM)] * 2 + [anywhere] * 8,
        out_specs=(here,) * 3,
        scratch_shapes=[
            pltpu.VMEM((STEPS,) + e_field.shape, F32),
            pltpu.VMEM(material.shape, jnp.int32),
            pltpu.VMEM(material.shape, F32),
            pltpu.VMEM(forward_dft.shape, BF16),
            pltpu.VMEM(interp_kernels.shape, F32),
            pltpu.VMEM((tile_cells, kernels * voxels), BF16),
            pltpu.VMEM((tile_cells, kernels * voxels), BF16),
            pltpu.VMEM(kernel_id.shape, jnp.int32),
            pltpu.VMEM(owner_map.shape, jnp.int32),
            pltpu.VMEM(slot_map.shape, jnp.int32),
            pltpu.VMEM((2 * STEPS * cells_y, 2 * forward_dft.shape[0] * cells_y), BF16),
            pltpu.VMEM((STEPS,) + e_field.shape, F32),
            pltpu.VMEM((depth // 128, cells_x, cells_y, 128), F32),
            pltpu.VMEM((STEPS, 2, cells_y, depth), F32),
            pltpu.VMEM((STEPS, 2, cells_y, depth), F32),
            pltpu.VMEM((STEPS, 2, cells_x, 1, depth), F32),
            pltpu.VMEM((STEPS, 2, cells_x, 1, depth), F32),
            pltpu.VMEM((STEPS, 2, cells_y, depth), F32),
            pltpu.VMEM((STEPS, 2, cells_x, 1, depth), F32),
            pltpu.VMEM((STEPS, 2, cells_x, 1, depth), F32),
            pltpu.VMEM((STEPS, 1, depth), F32),
            pltpu.VMEM((STEPS, 2, 1, depth), F32),
            pltpu.VMEM((count, capacity + 1, voxels), F32),
            pltpu.SemaphoreType.DMA((8,)),
            pltpu.SemaphoreType.DMA((6, STEPS)),
            pltpu.SemaphoreType.DMA((6, STEPS)),
            pltpu.SemaphoreType.REGULAR((32,)),
            pltpu.SemaphoreType.DMA((2,)),
        ],
        compiler_params=pltpu.CompilerParams(
            collective_id=0, has_side_effects=True, vmem_limit_bytes=60 * 2**20
        ),
    )(
        eps_table,
        phase_step,
        e_field,
        h_field,
        material,
        forward_dft,
        interp_kernels,
        kernel_id,
        owner_map,
        slot_map,
    )
    return pl.pallas_call(
        functools.partial(finish, capacity),
        out_shape=(field, field, jax.ShapeDtypeStruct((SLOTS, voxels), F32)),
        in_specs=[here] * 3,
        out_specs=(anywhere, anywhere, here),
        scratch_shapes=[pltpu.SemaphoreType.DMA((2,))],
        compiler_params=pltpu.CompilerParams(
            has_side_effects=True, vmem_limit_bytes=8 * 2**20
        ),
    )(*[pltpu.with_memory_space_constraint(part, pltpu.VMEM) for part in state])


def solution(mesh):
    return jax.shard_map(
        functools.partial(per_device, mesh.shape["gx"], mesh.shape["gy"]),
        mesh=mesh,
        in_specs=(
            P(None, "gx", "gy", None),
            P(None, "gx", "gy", None),
            P("gx", "gy", None),
            P(),
            P(None, None, None, "gx", "gy", None),
            P(),
            P(),
            P("gx", "gy"),
            P("gx", "gy"),
            P("gx", "gy"),
        ),
        out_specs=(P(None, "gx", "gy", None), P(None, "gx", "gy", None), P(("gx", "gy"), None)),
        check_vma=False,
    )
```

```python
import functools

import jax
import jax.numpy as jnp
from jax import lax
from jax.experimental import pallas as pl
from jax.experimental.pallas import tpu as pltpu
from jax.sharding import PartitionSpec as P

STEPS = 4
SLOTS = 64
COURANT = 0.5
UNROLL = 4

F32 = jnp.float32
BF16 = jnp.bfloat16
MESH = pl.DeviceIdType.MESH


def split2(value):
    high = value.astype(BF16)
    return high, (value - high.astype(F32)).astype(BF16)


def dot(lhs, rhs):
    return jnp.dot(lhs, rhs, preferred_element_type=F32)


def dot_rows(lhs, rhs):
    return lax.dot_general(lhs, rhs, (((0,), (0,)), ((), ())), preferred_element_type=F32)


def iota(shape, dim):
    return lax.broadcasted_iota(jnp.int32, shape, dim)


def as_row(values):
    rows, lanes = values.shape
    size = rows * lanes
    pick = (iota((rows, size), 1) // lanes == iota((rows, size), 0)).astype(BF16)
    spread = dot_rows(values.astype(F32).astype(BF16), pick)
    keep = iota((lanes, size), 0) == lax.rem(iota((lanes, size), 1), lanes)
    return jnp.sum(jnp.where(keep, spread, 0.0), axis=0, keepdims=True)


def kernel(
    size_x,
    size_y,
    capacity,
    eps_ref,
    phase_ref,
    e_in,
    h_in,
    mat_in,
    dft_in,
    kern_in,
    kid_in,
    owner_in,
    slot_in,
    last_elec,
    magn,
    got,
    elec_steps,
    mat,
    scale,
    dft,
    kern,
    kern_high,
    kern_low,
    kid,
    owner,
    slot,
    coefs,
    weights,
    sens,
    halo_ex,
    halo_hx,
    halo_ey,
    halo_hy,
    pack_hx,
    pack_ey,
    pack_hy,
    pack_corner,
    halo_corner,
    put,
    placement,
    kinds,
    in_sem,
    send_sem,
    recv_sem,
    round_sem,
    a2a_sem,
):
    count = size_x * size_y
    cells_x, cells_y, depth = mat.shape
    waves = dft.shape[0]
    tile_x, tile_y = kid.shape
    tiles = tile_x * tile_y
    kernels, tile_cells, voxels = kern.shape
    gx = lax.axis_index("gx")
    gy = lax.axis_index("gy")
    me = gx * size_y + gy

    elec = [elec_steps.at[step] for step in range(STEPS)] + [last_elec]

    loads = [
        pltpu.make_async_copy(source, target, in_sem.at[place])
        for place, (source, target) in enumerate(
            [
                (e_in, elec[0]),
                (h_in, magn),
                (mat_in, mat),
                (kid_in, kid),
                (owner_in, owner),
                (slot_in, slot),
                (kern_in, kern),
                (dft_in, dft),
            ]
        )
    ]
    for load in loads[:6]:
        load.start()

    first_x, last_x = gx > 0, gx < size_x - 1
    first_y, last_y = gy > 0, gy < size_y - 1
    partners = [
        (first_x, -1, 0),
        (last_x, 1, 0),
        (first_y, 0, -1),
        (last_y, 0, 1),
        (last_x & first_y, 1, -1),
        (first_x & last_y, -1, 1),
    ]
    def how_many(conditions):
        return sum(one.astype(jnp.int32) for one in conditions)

    barrier = pltpu.get_barrier_semaphore()
    for there, dx, dy in partners:

        @pl.when(there)
        def _():
            pl.semaphore_signal(
                barrier, inc=1, device_id=(gx + dx, gy + dy), device_id_type=MESH
            )

    def wait_partners():
        pl.semaphore_wait(barrier, how_many(there for there, _, _ in partners))

    rounds = []
    for axis, size in ((1, size_y), (0, size_x)):
        reach = 1
        while reach < size:
            rounds.append((axis, size, reach))
            reach *= 2

    def run_round(index):
        if not 0 <= index < len(rounds):
            return
        axis, size, reach = rounds[index]
        place = (gx, gy)[axis]
        sides = ((place >= reach, -reach), (place < size - reach, reach))
        for there, shift in sides:

            @pl.when(there)
            def _():
                peer = (gx + shift, gy) if axis == 0 else (gx, gy + shift)
                pl.semaphore_signal(
                    round_sem.at[index], inc=1, device_id=peer, device_id_type=MESH
                )

    def end_round(index):
        if not 0 <= index < len(rounds):
            return
        axis, size, reach = rounds[index]
        place = (gx, gy)[axis]
        peers = how_many((place >= reach, place < size - reach))
        pl.semaphore_wait(round_sem.at[index], peers)

    row_y = iota((cells_y, depth), 0)
    col_z = iota((cells_y, depth), 1)

    def y_up(v):
        return jnp.where(row_y == cells_y - 1, 0.0, pltpu.roll(v, cells_y - 1, 0))

    def z_up(v):
        return jnp.where(col_z == depth - 1, 0.0, pltpu.roll(v, depth - 1, 1))

    def y_down(v):
        return jnp.where(row_y == 0, 0.0, pltpu.roll(v, 1, 0))

    def z_down(v):
        return jnp.where(col_z == 0, 0.0, pltpu.roll(v, 1, 1))

    def h_plane(step, x, last):
        elec_now = elec[step]
        ex, ey, ez = elec_now[0, x], elec_now[1, x], elec_now[2, x]
        dx_ey = -ey if last else elec_now[1, x + 1] - ey
        dx_ez = -ez if last else elec_now[2, x + 1] - ez
        magn[0, x] = magn[0, x] - COURANT * ((y_up(ez) - ez) - (z_up(ey) - ey))
        magn[1, x] = magn[1, x] - COURANT * ((z_up(ex) - ex) - dx_ez)
        magn[2, x] = magn[2, x] - COURANT * (dx_ey - (y_up(ex) - ex))

    def e_plane(step, x, first):
        elec_now, elec_new = elec[step], elec[step + 1]
        hx, hy, hz = magn[0, x], magn[1, x], magn[2, x]
        dx_hy = hy if first else hy - magn[1, x - 1]
        dx_hz = hz if first else hz - magn[2, x - 1]
        factor = scale[x]
        elec_new[0, x] = elec_now[0, x] + factor * ((hz - y_down(hz)) - (hy - z_down(hy)))
        elec_new[1, x] = elec_now[1, x] + factor * ((hx - z_down(hx)) - dx_hz)
        elec_new[2, x] = elec_now[2, x] + factor * (dx_hy - (hx - y_down(hx)))

    def loop(low, high, body):
        def run(x, carry):
            body(x)
            return carry

        lax.fori_loop(low, high, run, 0, unroll=True)

    def h_interior(step):
        loop(0, cells_x - 1, lambda x: h_plane(step, x, False))

    def e_interior(step):
        e_plane(step, 0, True)
        loop(1, cells_x, lambda x: e_plane(step, x, False))

    def copy(kind, step, source, target, there, back, dx, dy):
        one = pltpu.make_async_remote_copy(
            src_ref=source,
            dst_ref=target,
            send_sem=send_sem.at[kind, step],
            recv_sem=recv_sem.at[kind, step],
            device_id=(gx + dx, gy + dy),
            device_id_type=MESH,
        )
        return there, back, one

    end_x, end_y = cells_x - 1, cells_y - 1
    top, bottom = pl.ds(0, 1), pl.ds(end_y, 1)
    sent = []

    def start(kind, step, *rest):
        there, _, one = copy(kind, step, *rest)
        sent.append((there, one))

        @pl.when(there)
        def _():
            one.start()

    def plans(step):
        corner = pack_corner.at[step]
        return {
            0: (pack_ey.at[step, 0, end_x], halo_corner.at[step, 0], last_x & first_y, first_x & last_y, 1, -1),
            1: (corner, halo_corner.at[step, 1], first_x & last_y, last_x & first_y, -1, 1),
            2: (elec[step].at[pl.ds(1, 2), 0], halo_ex.at[step], first_x, last_x, -1, 0),
            3: (pack_hx.at[step], halo_hx.at[step], last_x, first_x, 1, 0),
            4: (pack_ey.at[step], halo_ey.at[step], first_y, last_y, 0, -1),
            5: (pack_hy.at[step], halo_hy.at[step], last_y, first_y, 0, 1),
        }

    def begin(step, kind):
        start(kind, step, *plans(step)[kind])

    def arrive(step, kind):
        _, _, one = copy(kind, step, *plans(step)[kind])
        one.wait_recv()

    def send_elec(step):
        field = elec[step]
        pack_ey[step, 0] = field[0, :, top, :]
        pack_ey[step, 1] = field[2, :, top, :]
        pack_corner[step] = field[1, 0, bottom, :]
        begin(step, 0)
        begin(step, 1)
        begin(step, 2)
        begin(step, 4)

    def send_magn_x(step):
        h_plane(step, end_x, True)
        pack_hx[step, 0] = magn[1, end_x]
        pack_hx[step, 1] = magn[2, end_x]
        begin(step, 3)

    def send_magn_y(step):
        pack_hy[step, 0] = magn[0, :, bottom, :]
        pack_hy[step, 1] = magn[2, :, bottom, :]
        begin(step, 5)

    def receive(step):
        now, new = elec[step], elec[step + 1]
        col = iota((cells_x, 1, depth), 2)

        def grow(where, changes):
            terms = []
            for comp, change in changes:
                new[(comp, *where)] = new[(comp, *where)] + change
                if step == STEPS - 1:
                    terms.append(change * weights[(step, comp, *where)])
            for block in range(depth // 128 if terms else 0):
                lanes = sum(term[..., block * 128 : (block + 1) * 128] for term in terms)
                sens[(block, *where)] = sens[(block, *where)] + lanes

        @pl.when(last_y)
        def _():
            arrive(step, 4)
            where = (slice(None), bottom)
            d_hz = COURANT * halo_ey[step, 0]
            d_hx = -COURANT * halo_ey[step, 1]
            magn[(0, *where)] = magn[(0, *where)] + d_hx
            magn[(2, *where)] = magn[(2, *where)] + d_hz
            factor = scale[where]
            before = jnp.concatenate([jnp.zeros_like(d_hz[:1]), d_hz[:-1]], axis=0)
            z_before = jnp.where(col == 0, 0.0, pltpu.roll(d_hx, 1, 2))
            grow(
                where,
                (
                    (0, factor * d_hz),
                    (1, factor * ((d_hx - z_before) - (d_hz - before))),
                    (2, -factor * d_hx),
                ),
            )

        @pl.when(first_y)
        def _():
            arrive(step, 5)
            where = (slice(None), top)
            hx = halo_hy[step, 0] - COURANT * now[(2, *where)]
            hz = halo_hy[step, 1] + COURANT * now[(0, *where)]
            factor = scale[where]
            grow(where, ((0, -factor * hz), (2, factor * hx)))

        @pl.when(first_y & last_x)
        def _():
            arrive(step, 1)
            where = (end_x, top)
            grow(where, ((0, scale[where] * (COURANT * halo_corner[step, 1])),))

        @pl.when(last_x)
        def _():
            arrive(step, 2)
            d_hy = COURANT * halo_ex[step, 1]
            d_hz = -COURANT * halo_ex[step, 0]
            magn[1, end_x] = magn[1, end_x] + d_hy
            magn[2, end_x] = magn[2, end_x] + d_hz
            factor = scale[end_x]
            grow(
                (end_x,),
                (
                    (0, factor * ((d_hz - y_down(d_hz)) - (d_hy - z_down(d_hy)))),
                    (1, -factor * d_hz),
                    (2, factor * d_hy),
                ),
            )

        @pl.when(first_x & last_y)
        def _():
            arrive(step, 0)
            where = (0, bottom)
            grow(where, ((1, scale[where] * (COURANT * halo_corner[step, 0])),))

        @pl.when(first_x)
        def _():
            arrive(step, 3)
            hy = halo_hx[step, 0] + COURANT * now[2, 0]
            hz = halo_hx[step, 1] - COURANT * now[1, 0]
            factor = scale[0]
            grow((0,), ((1, factor * hz), (2, -factor * hy)))

    def wait_sent():
        for there, one in sent:

            @pl.when(there)
            def _():
                one.wait_send()

    def make_scale():
        def plane(x):
            kind = mat[x]
            eps = jnp.full(kind.shape, eps_ref[0], F32)
            for index in range(1, eps_ref.shape[0]):
                eps = jnp.where(kind == index, eps_ref[index], eps)
            scale[x] = COURANT / eps

        loop(0, cells_x, plane)

    def make_coefs():
        width = 2 * waves * cells_y
        column = iota((8, width), 1)
        wave = column // (2 * cells_y)
        phase = jnp.full((8, width), phase_ref[0], F32)
        for index in range(1, waves):
            phase = jnp.where(wave == index, phase_ref[index], phase)
        angle = phase * (iota((8, width), 0) + 1).astype(F32)
        imaginary = lax.rem(column // cells_y, 2) == 1
        values = jnp.where(imaginary, -jnp.sin(angle), jnp.cos(angle)) / float(waves * STEPS)
        own = iota((cells_y, width), 0) == lax.rem(iota((cells_y, width), 1), cells_y)
        table = jnp.concatenate(
            [jnp.where(own, values[step : step + 1], 0.0) for step in range(STEPS)], axis=0
        )
        coefs[...] = jnp.concatenate(split2(table), axis=0)

    def make_weights(low, high):
        half = STEPS * cells_y

        def plane(index):
            comp, x = lax.rem(index, 3), index // 3
            block = dft[:, :, comp, x].reshape(2 * waves * cells_y, depth)
            both = dot(coefs[...], block)
            weights[:, comp, x] = (both[:half] + both[half:]).reshape(STEPS, cells_y, depth)

        def several(index):
            for extra in range(UNROLL):
                plane(index * UNROLL + extra)

        loop(low, high, several)

    def add_sens(low, high):
        def plane(x):
            total = None
            for step in range(low, high):
                for comp in range(3):
                    term = elec[step + 1][comp, x] * weights[step, comp, x]
                    total = term if total is None else total + term
            for block in range(depth // 128):
                lanes = total[:, block * 128 : (block + 1) * 128]
                sens[block, x] = lanes if low == 0 else sens[block, x] + lanes

        loop(0, cells_x, plane)

    def as_column(values):
        pick = (iota((tiles, tile_x), 0) // tile_y == iota((tiles, tile_x), 1)).astype(BF16)
        spread = dot(pick, values.astype(F32).astype(BF16))
        keep = iota((tiles, tile_y), 1) == lax.rem(iota((tiles, tile_y), 0), tile_y)
        return jnp.sum(jnp.where(keep, spread, 0.0), axis=1, keepdims=True)

    def positions():
        own_row = as_row(owner[...])
        own_column = as_column(owner[...])
        earlier = (own_column == own_row) & (iota((tiles, tiles), 0) < iota((tiles, tiles), 1))
        rank = jnp.sum(jnp.where(earlier, 1.0, 0.0), axis=0, keepdims=True)
        return own_row, own_column, rank

    def label_slots():
        own_row, _, rank = positions()
        mine = (iota((count, tiles), 0).astype(F32) == own_row).astype(BF16)
        place = (iota((128, tiles), 0).astype(F32) == rank).astype(F32)
        labels = (place * (as_row(slot[...]) + 1.0)).astype(BF16)
        table = (
            lax.dot_general(mine, labels, (((1,), (1,)), ((), ())), preferred_element_type=F32)
            - 1.0
        )
        put[:, pl.ds(capacity, 1), :] = table.reshape(count, 1, 128)
        position = own_row * float(capacity) + rank
        placement[...] = (iota((count * capacity, tiles), 0).astype(F32) == position).astype(BF16)
        kinds[...] = jnp.broadcast_to(as_column(kid[...]), (tiles, voxels))

    def wait_all(buffer, place):
        part = buffer.at[pl.ds(0, count - 1)]
        pltpu.make_async_copy(part, part, a2a_sem.at[place]).wait()

    def make_kernels():
        for index in range(kernels):
            high, low = split2(kern[index])
            kern_high[:, index * voxels : (index + 1) * voxels] = high
            kern_low[:, index * voxels : (index + 1) * voxels] = low

    units = 3 * cells_x // UNROLL

    def share(part):
        make_weights(units * part // (STEPS - 1), units * (part + 1) // (STEPS - 1))

    loads[0].wait()
    wait_partners()
    for step in range(STEPS):
        send_elec(step)
        if step == 0:
            loads[1].wait()
            loads[7].start()
            loads[6].start()
        send_magn_x(step)
        h_interior(step)
        send_magn_y(step)
        end_round(2 * step - 1)
        run_round(2 * step)
        if step == 0:
            loads[2].wait()
            make_scale()
            make_coefs()
        e_interior(step)
        if step == 0:
            loads[7].wait()
        if step == 1:
            for place in (3, 4, 5):
                loads[place].wait()
            label_slots()
        if step == 2:
            loads[6].wait()
            make_kernels()
        if step < STEPS - 1:
            share(step)
        else:
            add_sens(0, STEPS)
        end_round(2 * step)
        run_round(2 * step + 1)
        receive(step)
    end_round(2 * STEPS - 1)
    for index in range(2 * STEPS, len(rounds)):
        run_round(index)
        end_round(index)

    parts = []
    for a in range(2):
        for b in range(2):
            for block in range(depth // 128):
                lanes = sens[block, pl.ds(a, cells_x // 2, 2), pl.ds(b, cells_y // 2, 2), :]
                parts.append(lanes.reshape(tiles, 128))
    high, low = split2(jnp.concatenate(parts, axis=1))
    big, small = kern_high[...], kern_low[...]
    total = dot(high, big) + (dot(low, big) + dot(high, small))
    restricted = jnp.zeros((tiles, voxels), F32)
    for index in range(kernels):
        restricted = restricted + jnp.where(
            kinds[...] == float(index), total[:, index * voxels : (index + 1) * voxels], 0.0
        )
    high, low = split2(restricted)
    put[:, pl.ds(0, capacity), :] = (dot(placement[...], high) + dot(placement[...], low)).reshape(
        count, capacity, voxels
    )
    got[me] = put[me]

    def push(step, carry):
        peer = lax.rem(me + step, count)
        pltpu.make_async_remote_copy(
            src_ref=put.at[peer],
            dst_ref=got.at[me],
            send_sem=a2a_sem.at[0],
            recv_sem=a2a_sem.at[1],
            device_id=(peer // size_y, lax.rem(peer, size_y)),
            device_id_type=MESH,
        ).start()
        return carry

    lax.fori_loop(1, count, push, 0)
    wait_sent()
    wait_all(got, 1)
    wait_all(put, 0)


def finish(capacity, elec, magn, got, e_out, h_out, grad_ref, sems):
    stores = [
        pltpu.make_async_copy(elec, e_out, sems.at[0]),
        pltpu.make_async_copy(magn, h_out, sems.at[1]),
    ]
    for store in stores:
        store.start()
    count, _, voxels = got.shape
    received = got[:, pl.ds(capacity, 1), :].reshape(count, 128)[:, :capacity]
    gather = (
        iota((SLOTS, count * capacity), 0).astype(F32) == as_row(received)
    ).astype(BF16)
    high, low = split2(got[:, pl.ds(0, capacity), :].reshape(count * capacity, voxels))
    grad_ref[...] = dot(gather, high) + dot(gather, low)
    for store in stores:
        store.wait()


def per_device(
    size_x,
    size_y,
    e_field,
    h_field,
    material,
    eps_table,
    forward_dft,
    phase_step,
    interp_kernels,
    kernel_id,
    owner_map,
    slot_map,
):
    count = size_x * size_y
    cells_x, cells_y, depth = material.shape
    kernels, tile_cells, voxels = interp_kernels.shape
    tiles = cells_x * cells_y // 4
    capacity = max(2, (2 * tiles + count - 1) // count)
    field = jax.ShapeDtypeStruct(e_field.shape, F32)
    anywhere = pl.BlockSpec(memory_space=pltpu.HBM)
    here = pl.BlockSpec(memory_space=pltpu.VMEM)
    state = pl.pallas_call(
        functools.partial(kernel, size_x, size_y, capacity),
        out_shape=(
            pltpu.VMEM(e_field.shape, F32),
            pltpu.VMEM(h_field.shape, F32),
            pltpu.VMEM((count, capacity + 1, voxels), F32),
        ),
        in_specs=[pl.BlockSpec(memory_space=pltpu.SMEM)] * 2 + [anywhere] * 8,
        out_specs=(here,) * 3,
        scratch_shapes=[
            pltpu.VMEM((STEPS,) + e_field.shape, F32),
            pltpu.VMEM(material.shape, jnp.int32),
            pltpu.VMEM(material.shape, F32),
            pltpu.VMEM(forward_dft.shape, BF16),
            pltpu.VMEM(interp_kernels.shape, F32),
            pltpu.VMEM((tile_cells, kernels * voxels), BF16),
            pltpu.VMEM((tile_cells, kernels * voxels), BF16),
            pltpu.VMEM(kernel_id.shape, jnp.int32),
            pltpu.VMEM(owner_map.shape, jnp.int32),
            pltpu.VMEM(slot_map.shape, jnp.int32),
            pltpu.VMEM((2 * STEPS * cells_y, 2 * forward_dft.shape[0] * cells_y), BF16),
            pltpu.VMEM((STEPS,) + e_field.shape, F32),
            pltpu.VMEM((depth // 128, cells_x, cells_y, 128), F32),
            pltpu.VMEM((STEPS, 2, cells_y, depth), F32),
            pltpu.VMEM((STEPS, 2, cells_y, depth), F32),
            pltpu.VMEM((STEPS, 2, cells_x, 1, depth), F32),
            pltpu.VMEM((STEPS, 2, cells_x, 1, depth), F32),
            pltpu.VMEM((STEPS, 2, cells_y, depth), F32),
            pltpu.VMEM((STEPS, 2, cells_x, 1, depth), F32),
            pltpu.VMEM((STEPS, 2, cells_x, 1, depth), F32),
            pltpu.VMEM((STEPS, 1, depth), F32),
            pltpu.VMEM((STEPS, 2, 1, depth), F32),
            pltpu.VMEM((count, capacity + 1, voxels), F32),
            pltpu.VMEM((count * capacity, tiles), BF16),
            pltpu.VMEM((tiles, voxels), F32),
            pltpu.SemaphoreType.DMA((8,)),
            pltpu.SemaphoreType.DMA((6, STEPS)),
            pltpu.SemaphoreType.DMA((6, STEPS)),
            pltpu.SemaphoreType.REGULAR((32,)),
            pltpu.SemaphoreType.DMA((2,)),
        ],
        compiler_params=pltpu.CompilerParams(
            collective_id=0, has_side_effects=True, vmem_limit_bytes=60 * 2**20
        ),
    )(
        eps_table,
        phase_step,
        e_field,
        h_field,
        material,
        forward_dft,
        interp_kernels,
        kernel_id,
        owner_map,
        slot_map,
    )
    return pl.pallas_call(
        functools.partial(finish, capacity),
        out_shape=(field, field, jax.ShapeDtypeStruct((SLOTS, voxels), F32)),
        in_specs=[here] * 3,
        out_specs=(anywhere, anywhere, here),
        scratch_shapes=[pltpu.SemaphoreType.DMA((2,))],
        compiler_params=pltpu.CompilerParams(
            has_side_effects=True, vmem_limit_bytes=8 * 2**20
        ),
    )(*[pltpu.with_memory_space_constraint(part, pltpu.VMEM) for part in state])


def solution(mesh):
    return jax.shard_map(
        functools.partial(per_device, mesh.shape["gx"], mesh.shape["gy"]),
        mesh=mesh,
        in_specs=(
            P(None, "gx", "gy", None),
            P(None, "gx", "gy", None),
            P("gx", "gy", None),
            P(),
            P(None, None, None, "gx", "gy", None),
            P(),
            P(),
            P("gx", "gy"),
            P("gx", "gy"),
            P("gx", "gy"),
        ),
        out_specs=(P(None, "gx", "gy", None), P(None, "gx", "gy", None), P(("gx", "gy"), None)),
        check_vma=False,
    )
```

```python
import functools

import jax
import jax.numpy as jnp
from jax import lax
from jax.experimental import pallas as pl
from jax.experimental.pallas import tpu as pltpu
from jax.sharding import PartitionSpec as P

STEPS = 4
SLOTS = 64
COURANT = 0.5
UNROLL = 4

F32 = jnp.float32
BF16 = jnp.bfloat16
MESH = pl.DeviceIdType.MESH


def split2(value):
    high = value.astype(BF16)
    return high, (value - high.astype(F32)).astype(BF16)


def dot(lhs, rhs):
    return jnp.dot(lhs, rhs, preferred_element_type=F32)


def dot_rows(lhs, rhs):
    return lax.dot_general(lhs, rhs, (((0,), (0,)), ((), ())), preferred_element_type=F32)


def iota(shape, dim):
    return lax.broadcasted_iota(jnp.int32, shape, dim)


def as_row(values):
    rows, lanes = values.shape
    size = rows * lanes
    pick = (iota((rows, size), 1) // lanes == iota((rows, size), 0)).astype(BF16)
    spread = dot_rows(values.astype(F32).astype(BF16), pick)
    keep = iota((lanes, size), 0) == lax.rem(iota((lanes, size), 1), lanes)
    return jnp.sum(jnp.where(keep, spread, 0.0), axis=0, keepdims=True)


def kernel(
    size_x,
    size_y,
    capacity,
    eps_ref,
    phase_ref,
    e_in,
    h_in,
    mat_in,
    dft_in,
    kern_in,
    kid_in,
    owner_in,
    slot_in,
    last_elec,
    magn,
    got,
    elec_steps,
    mat,
    scale,
    dft,
    kern,
    kern_high,
    kern_low,
    kid,
    owner,
    slot,
    coefs,
    weights,
    sens,
    halo_ex,
    halo_hx,
    halo_ey,
    halo_hy,
    pack_hx,
    pack_ey,
    pack_hy,
    pack_corner,
    halo_corner,
    put,
    placement,
    kinds,
    in_sem,
    send_sem,
    recv_sem,
    round_sem,
    a2a_sem,
):
    count = size_x * size_y
    cells_x, cells_y, depth = mat.shape
    waves = dft.shape[0]
    tile_x, tile_y = kid.shape
    tiles = tile_x * tile_y
    kernels, tile_cells, voxels = kern.shape
    gx = lax.axis_index("gx")
    gy = lax.axis_index("gy")
    me = gx * size_y + gy

    elec = [elec_steps.at[step] for step in range(STEPS)] + [last_elec]

    loads = [
        pltpu.make_async_copy(source, target, in_sem.at[place])
        for place, (source, target) in enumerate(
            [
                (e_in.at[:, pl.ds(1, cells_x - 2)], elec[0].at[:, pl.ds(1, cells_x - 2)]),
                (h_in.at[:, pl.ds(0, cells_x - 1)], magn.at[:, pl.ds(0, cells_x - 1)]),
                (mat_in, mat),
                (kid_in, kid),
                (owner_in, owner),
                (slot_in, slot),
                (kern_in, kern),
                (dft_in, dft),
                (e_in.at[:, 0], elec[0].at[:, 0]),
                (e_in.at[:, cells_x - 1], elec[0].at[:, cells_x - 1]),
                (h_in.at[:, cells_x - 1], magn.at[:, cells_x - 1]),
            ]
        )
    ]
    for load in loads[8:] + loads[:6]:
        load.start()

    first_x, last_x = gx > 0, gx < size_x - 1
    first_y, last_y = gy > 0, gy < size_y - 1
    partners = [
        (first_x, -1, 0),
        (last_x, 1, 0),
        (first_y, 0, -1),
        (last_y, 0, 1),
        (last_x & first_y, 1, -1),
        (first_x & last_y, -1, 1),
    ]
    def how_many(conditions):
        return sum(one.astype(jnp.int32) for one in conditions)

    barrier = pltpu.get_barrier_semaphore()
    for there, dx, dy in partners:

        @pl.when(there)
        def _():
            pl.semaphore_signal(
                barrier, inc=1, device_id=(gx + dx, gy + dy), device_id_type=MESH
            )

    def wait_partners():
        pl.semaphore_wait(barrier, how_many(there for there, _, _ in partners))

    rounds = []
    for axis, size in ((1, size_y), (0, size_x)):
        reach = 1
        while reach < size:
            rounds.append((axis, size, reach))
            reach *= 2

    def run_round(index):
        if not 0 <= index < len(rounds):
            return
        axis, size, reach = rounds[index]
        place = (gx, gy)[axis]
        sides = ((place >= reach, -reach), (place < size - reach, reach))
        for there, shift in sides:

            @pl.when(there)
            def _():
                peer = (gx + shift, gy) if axis == 0 else (gx, gy + shift)
                pl.semaphore_signal(
                    round_sem.at[index], inc=1, device_id=peer, device_id_type=MESH
                )

    def end_round(index):
        if not 0 <= index < len(rounds):
            return
        axis, size, reach = rounds[index]
        place = (gx, gy)[axis]
        peers = how_many((place >= reach, place < size - reach))
        pl.semaphore_wait(round_sem.at[index], peers)

    row_y = iota((cells_y, depth), 0)
    col_z = iota((cells_y, depth), 1)

    def y_up(v):
        return jnp.where(row_y == cells_y - 1, 0.0, pltpu.roll(v, cells_y - 1, 0))

    def z_up(v):
        return jnp.where(col_z == depth - 1, 0.0, pltpu.roll(v, depth - 1, 1))

    def y_down(v):
        return jnp.where(row_y == 0, 0.0, pltpu.roll(v, 1, 0))

    def z_down(v):
        return jnp.where(col_z == 0, 0.0, pltpu.roll(v, 1, 1))

    def h_plane(step, x, last):
        elec_now = elec[step]
        ex, ey, ez = elec_now[0, x], elec_now[1, x], elec_now[2, x]
        dx_ey = -ey if last else elec_now[1, x + 1] - ey
        dx_ez = -ez if last else elec_now[2, x + 1] - ez
        magn[0, x] = magn[0, x] - COURANT * ((y_up(ez) - ez) - (z_up(ey) - ey))
        magn[1, x] = magn[1, x] - COURANT * ((z_up(ex) - ex) - dx_ez)
        magn[2, x] = magn[2, x] - COURANT * (dx_ey - (y_up(ex) - ex))

    def e_plane(step, x, first):
        elec_now, elec_new = elec[step], elec[step + 1]
        hx, hy, hz = magn[0, x], magn[1, x], magn[2, x]
        dx_hy = hy if first else hy - magn[1, x - 1]
        dx_hz = hz if first else hz - magn[2, x - 1]
        factor = scale[x]
        elec_new[0, x] = elec_now[0, x] + factor * ((hz - y_down(hz)) - (hy - z_down(hy)))
        elec_new[1, x] = elec_now[1, x] + factor * ((hx - z_down(hx)) - dx_hz)
        elec_new[2, x] = elec_now[2, x] + factor * (dx_hy - (hx - y_down(hx)))

    def loop(low, high, body):
        def run(x, carry):
            body(x)
            return carry

        lax.fori_loop(low, high, run, 0, unroll=True)

    def h_interior(step):
        loop(0, cells_x - 1, lambda x: h_plane(step, x, False))

    def e_interior(step):
        e_plane(step, 0, True)
        loop(1, cells_x, lambda x: e_plane(step, x, False))

    def copy(kind, step, source, target, there, back, dx, dy):
        one = pltpu.make_async_remote_copy(
            src_ref=source,
            dst_ref=target,
            send_sem=send_sem.at[kind, step],
            recv_sem=recv_sem.at[kind, step],
            device_id=(gx + dx, gy + dy),
            device_id_type=MESH,
        )
        return there, back, one

    end_x, end_y = cells_x - 1, cells_y - 1
    top, bottom = pl.ds(0, 1), pl.ds(end_y, 1)
    sent = []
    gate_x, gate_y = first_x.astype(F32), first_y.astype(F32)

    def start(kind, step, *rest):
        there, _, one = copy(kind, step, *rest)
        sent.append((there, one))

        @pl.when(there)
        def _():
            one.start()

    def plans(step):
        corner = pack_corner.at[step]
        return {
            0: (corner.at[0], halo_corner.at[step, 0], last_x & first_y, first_x & last_y, 1, -1),
            1: (corner.at[1], halo_corner.at[step, 1], first_x & last_y, last_x & first_y, -1, 1),
            2: (elec[step].at[pl.ds(1, 2), 0], halo_ex.at[step], first_x, last_x, -1, 0),
            3: (pack_hx.at[step], halo_hx.at[step], last_x, first_x, 1, 0),
            4: (pack_ey.at[step], halo_ey.at[step], first_y, last_y, 0, -1),
            5: (pack_hy.at[step], halo_hy.at[step], last_y, first_y, 0, 1),
        }

    def begin(step, kind):
        start(kind, step, *plans(step)[kind])

    def arrive(step, kind):
        _, back, one = copy(kind, step, *plans(step)[kind])

        @pl.when(back)
        def _():
            one.wait_recv()

    def send_elec_x(step):
        pack_corner[step, 0] = elec[step][0, end_x, top, :]
        pack_corner[step, 1] = elec[step][1, 0, bottom, :]
        begin(step, 0)
        begin(step, 1)
        begin(step, 2)

    def send_elec_y(step):
        pack_ey[step, 0] = elec[step][0, :, top, :]
        pack_ey[step, 1] = elec[step][2, :, top, :]
        begin(step, 4)

    def send_magn_x(step):
        h_plane(step, end_x, True)
        pack_hx[step, 0] = magn[1, end_x]
        pack_hx[step, 1] = magn[2, end_x]
        begin(step, 3)

    def send_magn_y(step):
        pack_hy[step, 0] = magn[0, :, bottom, :]
        pack_hy[step, 1] = magn[2, :, bottom, :]
        begin(step, 5)

    def receive(step):
        now, new = elec[step], elec[step + 1]
        col = iota((cells_x, 1, depth), 2)

        def grow(where, changes):
            terms = []
            for comp, change in changes:
                new[(comp, *where)] = new[(comp, *where)] + change
                if step == STEPS - 1:
                    terms.append(change * weights[(step, comp, *where)])
            for block in range(depth // 128 if terms else 0):
                lanes = sum(term[..., block * 128 : (block + 1) * 128] for term in terms)
                sens[(block, *where)] = sens[(block, *where)] + lanes

        arrive(step, 4)
        arrive(step, 5)
        low, high = (slice(None), top), (slice(None), bottom)
        d_hz = COURANT * halo_ey[step, 0]
        d_hx = -COURANT * halo_ey[step, 1]
        magn[(0, *high)] = magn[(0, *high)] + d_hx
        magn[(2, *high)] = magn[(2, *high)] + d_hz
        before = jnp.concatenate([jnp.zeros_like(d_hz[:1]), d_hz[:-1]], axis=0)
        z_before = jnp.where(col == 0, 0.0, pltpu.roll(d_hx, 1, 2))
        factor = scale[high]
        grow(
            high,
            (
                (0, factor * d_hz),
                (1, factor * ((d_hx - z_before) - (d_hz - before))),
                (2, -factor * d_hx),
            ),
        )
        hx = gate_y * (halo_hy[step, 0] - COURANT * now[(2, *low)])
        hz = gate_y * (halo_hy[step, 1] + COURANT * now[(0, *low)])
        factor = scale[low]
        grow(low, ((0, -factor * hz), (2, factor * hx)))

        for kind in range(4):
            arrive(step, kind)
        corner = COURANT * halo_corner[step]
        hy = gate_x * (halo_hx[step, 0] + COURANT * now[2, 0])
        hz = gate_x * (halo_hx[step, 1] - COURANT * now[1, 0])
        hz = hz + jnp.where(row_y == end_y, corner[0], 0.0)
        factor = scale[0]
        grow((0,), ((1, factor * hz), (2, -factor * hy)))
        d_hy = COURANT * halo_ex[step, 1]
        d_hz = -COURANT * halo_ex[step, 0]
        magn[1, end_x] = magn[1, end_x] + d_hy
        magn[2, end_x] = magn[2, end_x] + d_hz
        y_before = jnp.where(row_y == 0, -corner[1], pltpu.roll(d_hz, 1, 0))
        factor = scale[end_x]
        grow(
            (end_x,),
            (
                (0, factor * ((d_hz - y_before) - (d_hy - z_down(d_hy)))),
                (1, -factor * d_hz),
                (2, factor * d_hy),
            ),
        )

    def clear_missing():
        for missing, buffer in (
            (gx == size_x - 1, halo_ex),
            (gx == 0, halo_hx),
            (gy == size_y - 1, halo_ey),
            (gy == 0, halo_hy),
            ((gx == 0) | (gy == size_y - 1), halo_corner.at[:, 0]),
            ((gx == size_x - 1) | (gy == 0), halo_corner.at[:, 1]),
        ):

            @pl.when(missing)
            def _():
                buffer[...] = jnp.zeros(buffer.shape, F32)

    def wait_sent():
        for there, one in sent:

            @pl.when(there)
            def _():
                one.wait_send()

    def make_scale():
        def plane(x):
            kind = mat[x]
            eps = jnp.full(kind.shape, eps_ref[0], F32)
            for index in range(1, eps_ref.shape[0]):
                eps = jnp.where(kind == index, eps_ref[index], eps)
            scale[x] = COURANT / eps

        loop(0, cells_x, plane)

    def make_coefs():
        width = 2 * waves * cells_y
        column = iota((8, width), 1)
        wave = column // (2 * cells_y)
        phase = jnp.full((8, width), phase_ref[0], F32)
        for index in range(1, waves):
            phase = jnp.where(wave == index, phase_ref[index], phase)
        angle = phase * (iota((8, width), 0) + 1).astype(F32)
        imaginary = lax.rem(column // cells_y, 2) == 1
        values = jnp.where(imaginary, -jnp.sin(angle), jnp.cos(angle)) / float(waves * STEPS)
        own = iota((cells_y, width), 0) == lax.rem(iota((cells_y, width), 1), cells_y)
        table = jnp.concatenate(
            [jnp.where(own, values[step : step + 1], 0.0) for step in range(STEPS)], axis=0
        )
        coefs[...] = jnp.concatenate(split2(table), axis=0)

    def make_weights(low, high):
        half = STEPS * cells_y

        def plane(index):
            comp, x = lax.rem(index, 3), index // 3
            block = dft[:, :, comp, x].reshape(2 * waves * cells_y, depth)
            both = dot(coefs[...], block)
            weights[:, comp, x] = (both[:half] + both[half:]).reshape(STEPS, cells_y, depth)

        def several(index):
            for extra in range(UNROLL):
                plane(index * UNROLL + extra)

        loop(low, high, several)

    def add_sens(low, high):
        def plane(x):
            total = None
            for step in range(low, high):
                for comp in range(3):
                    term = elec[step + 1][comp, x] * weights[step, comp, x]
                    total = term if total is None else total + term
            for block in range(depth // 128):
                lanes = total[:, block * 128 : (block + 1) * 128]
                sens[block, x] = lanes if low == 0 else sens[block, x] + lanes

        loop(0, cells_x, plane)

    def as_column(values):
        pick = (iota((tiles, tile_x), 0) // tile_y == iota((tiles, tile_x), 1)).astype(BF16)
        spread = dot(pick, values.astype(F32).astype(BF16))
        keep = iota((tiles, tile_y), 1) == lax.rem(iota((tiles, tile_y), 0), tile_y)
        return jnp.sum(jnp.where(keep, spread, 0.0), axis=1, keepdims=True)

    def positions():
        own_row = as_row(owner[...])
        own_column = as_column(owner[...])
        earlier = (own_column == own_row) & (iota((tiles, tiles), 0) < iota((tiles, tiles), 1))
        rank = jnp.sum(jnp.where(earlier, 1.0, 0.0), axis=0, keepdims=True)
        return own_row, own_column, rank

    def label_slots():
        own_row, _, rank = positions()
        mine = (iota((count, tiles), 0).astype(F32) == own_row).astype(BF16)
        place = (iota((128, tiles), 0).astype(F32) == rank).astype(F32)
        labels = (place * (as_row(slot[...]) + 1.0)).astype(BF16)
        table = (
            lax.dot_general(mine, labels, (((1,), (1,)), ((), ())), preferred_element_type=F32)
            - 1.0
        )
        put[:, pl.ds(capacity, 1), :] = table.reshape(count, 1, 128)
        position = own_row * float(capacity) + rank
        placement[...] = (iota((count * capacity, tiles), 0).astype(F32) == position).astype(BF16)
        kinds[...] = jnp.broadcast_to(as_column(kid[...]), (tiles, voxels))

    def wait_all(buffer, place):
        part = buffer.at[pl.ds(0, count - 1)]
        pltpu.make_async_copy(part, part, a2a_sem.at[place]).wait()

    def make_kernels():
        for index in range(kernels):
            high, low = split2(kern[index])
            kern_high[:, index * voxels : (index + 1) * voxels] = high
            kern_low[:, index * voxels : (index + 1) * voxels] = low

    units = 3 * cells_x // UNROLL

    def share(part):
        make_weights(units * part // (STEPS - 1), units * (part + 1) // (STEPS - 1))

    loads[8].wait()
    loads[9].wait()
    wait_partners()
    for step in range(STEPS):
        send_elec_x(step)
        if step == 0:
            loads[10].wait()
        send_magn_x(step)
        if step == 0:
            loads[0].wait()
        send_elec_y(step)
        if step == 0:
            loads[1].wait()
        h_interior(step)
        send_magn_y(step)
        if step == 0:
            loads[7].start()
            clear_missing()
        if step == 1:
            loads[6].start()
        end_round(2 * step - 1)
        run_round(2 * step)
        if step == 0:
            loads[2].wait()
            make_scale()
            make_coefs()
        e_interior(step)
        if step == 1:
            loads[7].wait()
            for place in (3, 4, 5):
                loads[place].wait()
            label_slots()
        if step == 2:
            loads[6].wait()
            make_kernels()
        if step > 0:
            share(step - 1)
        if step == STEPS - 1:
            add_sens(0, STEPS)
        end_round(2 * step)
        run_round(2 * step + 1)
        receive(step)
    end_round(2 * STEPS - 1)
    for index in range(2 * STEPS, len(rounds)):
        run_round(index)
        end_round(index)

    parts = []
    for a in range(2):
        for b in range(2):
            for block in range(depth // 128):
                lanes = sens[block, pl.ds(a, cells_x // 2, 2), pl.ds(b, cells_y // 2, 2), :]
                parts.append(lanes.reshape(tiles, 128))
    high, low = split2(jnp.concatenate(parts, axis=1))
    big, small = kern_high[...], kern_low[...]
    total = dot(high, big) + (dot(low, big) + dot(high, small))
    restricted = jnp.zeros((tiles, voxels), F32)
    for index in range(kernels):
        restricted = restricted + jnp.where(
            kinds[...] == float(index), total[:, index * voxels : (index + 1) * voxels], 0.0
        )
    high, low = split2(restricted)
    put[:, pl.ds(0, capacity), :] = (dot(placement[...], high) + dot(placement[...], low)).reshape(
        count, capacity, voxels
    )
    got[me] = put[me]

    def push(step, carry):
        peer = lax.rem(me + step, count)
        pltpu.make_async_remote_copy(
            src_ref=put.at[peer],
            dst_ref=got.at[me],
            send_sem=a2a_sem.at[0],
            recv_sem=a2a_sem.at[1],
            device_id=(peer // size_y, lax.rem(peer, size_y)),
            device_id_type=MESH,
        ).start()
        return carry

    lax.fori_loop(1, count, push, 0)
    wait_sent()
    wait_all(got, 1)
    wait_all(put, 0)


def finish(capacity, elec, magn, got, e_out, h_out, grad_ref, sems):
    stores = [
        pltpu.make_async_copy(elec, e_out, sems.at[0]),
        pltpu.make_async_copy(magn, h_out, sems.at[1]),
    ]
    for store in stores:
        store.start()
    count, _, voxels = got.shape
    received = got[:, pl.ds(capacity, 1), :].reshape(count, 128)[:, :capacity]
    gather = (
        iota((SLOTS, count * capacity), 0).astype(F32) == as_row(received)
    ).astype(BF16)
    high, low = split2(got[:, pl.ds(0, capacity), :].reshape(count * capacity, voxels))
    grad_ref[...] = dot(gather, high) + dot(gather, low)
    for store in stores:
        store.wait()


def per_device(
    size_x,
    size_y,
    e_field,
    h_field,
    material,
    eps_table,
    forward_dft,
    phase_step,
    interp_kernels,
    kernel_id,
    owner_map,
    slot_map,
):
    count = size_x * size_y
    cells_x, cells_y, depth = material.shape
    kernels, tile_cells, voxels = interp_kernels.shape
    tiles = cells_x * cells_y // 4
    capacity = max(2, (2 * tiles + count - 1) // count)
    field = jax.ShapeDtypeStruct(e_field.shape, F32)
    anywhere = pl.BlockSpec(memory_space=pltpu.HBM)
    here = pl.BlockSpec(memory_space=pltpu.VMEM)
    state = pl.pallas_call(
        functools.partial(kernel, size_x, size_y, capacity),
        out_shape=(
            pltpu.VMEM(e_field.shape, F32),
            pltpu.VMEM(h_field.shape, F32),
            pltpu.VMEM((count, capacity + 1, voxels), F32),
        ),
        in_specs=[pl.BlockSpec(memory_space=pltpu.SMEM)] * 2 + [anywhere] * 8,
        out_specs=(here,) * 3,
        scratch_shapes=[
            pltpu.VMEM((STEPS,) + e_field.shape, F32),
            pltpu.VMEM(material.shape, jnp.int32),
            pltpu.VMEM(material.shape, F32),
            pltpu.VMEM(forward_dft.shape, BF16),
            pltpu.VMEM(interp_kernels.shape, F32),
            pltpu.VMEM((tile_cells, kernels * voxels), BF16),
            pltpu.VMEM((tile_cells, kernels * voxels), BF16),
            pltpu.VMEM(kernel_id.shape, jnp.int32),
            pltpu.VMEM(owner_map.shape, jnp.int32),
            pltpu.VMEM(slot_map.shape, jnp.int32),
            pltpu.VMEM((2 * STEPS * cells_y, 2 * forward_dft.shape[0] * cells_y), BF16),
            pltpu.VMEM((STEPS,) + e_field.shape, F32),
            pltpu.VMEM((depth // 128, cells_x, cells_y, 128), F32),
            pltpu.VMEM((STEPS, 2, cells_y, depth), F32),
            pltpu.VMEM((STEPS, 2, cells_y, depth), F32),
            pltpu.VMEM((STEPS, 2, cells_x, 1, depth), F32),
            pltpu.VMEM((STEPS, 2, cells_x, 1, depth), F32),
            pltpu.VMEM((STEPS, 2, cells_y, depth), F32),
            pltpu.VMEM((STEPS, 2, cells_x, 1, depth), F32),
            pltpu.VMEM((STEPS, 2, cells_x, 1, depth), F32),
            pltpu.VMEM((STEPS, 2, 1, depth), F32),
            pltpu.VMEM((STEPS, 2, 1, depth), F32),
            pltpu.VMEM((count, capacity + 1, voxels), F32),
            pltpu.VMEM((count * capacity, tiles), BF16),
            pltpu.VMEM((tiles, voxels), F32),
            pltpu.SemaphoreType.DMA((11,)),
            pltpu.SemaphoreType.DMA((6, STEPS)),
            pltpu.SemaphoreType.DMA((6, STEPS)),
            pltpu.SemaphoreType.REGULAR((32,)),
            pltpu.SemaphoreType.DMA((2,)),
        ],
        compiler_params=pltpu.CompilerParams(
            collective_id=0, has_side_effects=True, vmem_limit_bytes=60 * 2**20
        ),
    )(
        eps_table,
        phase_step,
        e_field,
        h_field,
        material,
        forward_dft,
        interp_kernels,
        kernel_id,
        owner_map,
        slot_map,
    )
    return pl.pallas_call(
        functools.partial(finish, capacity),
        out_shape=(field, field, jax.ShapeDtypeStruct((SLOTS, voxels), F32)),
        in_specs=[here] * 3,
        out_specs=(anywhere, anywhere, here),
        scratch_shapes=[pltpu.SemaphoreType.DMA((2,))],
        compiler_params=pltpu.CompilerParams(
            has_side_effects=True, vmem_limit_bytes=8 * 2**20
        ),
    )(*[pltpu.with_memory_space_constraint(part, pltpu.VMEM) for part in state])


def solution(mesh):
    return jax.shard_map(
        functools.partial(per_device, mesh.shape["gx"], mesh.shape["gy"]),
        mesh=mesh,
        in_specs=(
            P(None, "gx", "gy", None),
            P(None, "gx", "gy", None),
            P("gx", "gy", None),
            P(),
            P(None, None, None, "gx", "gy", None),
            P(),
            P(),
            P("gx", "gy"),
            P("gx", "gy"),
            P("gx", "gy"),
        ),
        out_specs=(P(None, "gx", "gy", None), P(None, "gx", "gy", None), P(("gx", "gy"), None)),
        check_vma=False,
    )
```

```python
import functools

import jax
import jax.numpy as jnp
from jax import lax
from jax.experimental import pallas as pl
from jax.experimental.pallas import tpu as pltpu
from jax.sharding import PartitionSpec as P

STEPS = 4
SLOTS = 64
COURANT = 0.5
UNROLL = 4

F32 = jnp.float32
BF16 = jnp.bfloat16
MESH = pl.DeviceIdType.MESH


def split2(value):
    high = value.astype(BF16)
    return high, (value - high.astype(F32)).astype(BF16)


def dot(lhs, rhs):
    return jnp.dot(lhs, rhs, preferred_element_type=F32)


def dot_rows(lhs, rhs):
    return lax.dot_general(lhs, rhs, (((0,), (0,)), ((), ())), preferred_element_type=F32)


def iota(shape, dim):
    return lax.broadcasted_iota(jnp.int32, shape, dim)


def as_row(values):
    rows, lanes = values.shape
    size = rows * lanes
    pick = (iota((rows, size), 1) // lanes == iota((rows, size), 0)).astype(BF16)
    spread = dot_rows(values.astype(F32).astype(BF16), pick)
    keep = iota((lanes, size), 0) == lax.rem(iota((lanes, size), 1), lanes)
    return jnp.sum(jnp.where(keep, spread, 0.0), axis=0, keepdims=True)


def kernel(
    size_x,
    size_y,
    capacity,
    eps_ref,
    phase_ref,
    e_in,
    h_in,
    mat_in,
    dft_in,
    kern_in,
    kid_in,
    owner_in,
    slot_in,
    last_elec,
    magn,
    got,
    elec_steps,
    mat,
    scale,
    dft,
    kern,
    kern_high,
    kern_low,
    kid,
    owner,
    slot,
    coefs,
    weights,
    sens,
    halo_ex,
    halo_hx,
    halo_ey,
    halo_hy,
    pack_hx,
    pack_ey,
    pack_hy,
    pack_corner,
    halo_corner,
    put,
    placement,
    kinds,
    in_sem,
    send_sem,
    recv_sem,
    round_sem,
    a2a_sem,
):
    count = size_x * size_y
    cells_x, cells_y, depth = mat.shape
    waves = dft.shape[0]
    tile_x, tile_y = kid.shape
    tiles = tile_x * tile_y
    kernels, tile_cells, voxels = kern.shape
    gx = lax.axis_index("gx")
    gy = lax.axis_index("gy")
    me = gx * size_y + gy

    elec = [elec_steps.at[step] for step in range(STEPS)] + [last_elec]

    loads = [
        pltpu.make_async_copy(source, target, in_sem.at[place])
        for place, (source, target) in enumerate(
            [
                (e_in.at[:, pl.ds(1, cells_x - 2)], elec[0].at[:, pl.ds(1, cells_x - 2)]),
                (h_in.at[:, pl.ds(0, cells_x - 1)], magn.at[:, pl.ds(0, cells_x - 1)]),
                (mat_in, mat),
                (kid_in, kid),
                (owner_in, owner),
                (slot_in, slot),
                (kern_in, kern),
                (dft_in, dft),
                (e_in.at[:, 0], elec[0].at[:, 0]),
                (e_in.at[:, cells_x - 1], elec[0].at[:, cells_x - 1]),
                (h_in.at[:, cells_x - 1], magn.at[:, cells_x - 1]),
            ]
        )
    ]
    for load in loads[8:] + loads[:6]:
        load.start()

    first_x, last_x = gx > 0, gx < size_x - 1
    first_y, last_y = gy > 0, gy < size_y - 1
    partners = [
        (first_x, -1, 0),
        (last_x, 1, 0),
        (first_y, 0, -1),
        (last_y, 0, 1),
        (last_x & first_y, 1, -1),
        (first_x & last_y, -1, 1),
    ]
    def how_many(conditions):
        return sum(one.astype(jnp.int32) for one in conditions)

    barrier = pltpu.get_barrier_semaphore()
    for there, dx, dy in partners:

        @pl.when(there)
        def _():
            pl.semaphore_signal(
                barrier, inc=1, device_id=(gx + dx, gy + dy), device_id_type=MESH
            )

    def wait_partners():
        pl.semaphore_wait(barrier, how_many(there for there, _, _ in partners))

    rounds = []
    for axis, size in ((1, size_y), (0, size_x)):
        reach = 1
        while reach < size:
            rounds.append((axis, size, reach))
            reach *= 2

    def run_round(index):
        if not 0 <= index < len(rounds):
            return
        axis, size, reach = rounds[index]
        place = (gx, gy)[axis]
        sides = ((place >= reach, -reach), (place < size - reach, reach))
        for there, shift in sides:

            @pl.when(there)
            def _():
                peer = (gx + shift, gy) if axis == 0 else (gx, gy + shift)
                pl.semaphore_signal(
                    round_sem.at[index], inc=1, device_id=peer, device_id_type=MESH
                )

    def end_round(index):
        if not 0 <= index < len(rounds):
            return
        axis, size, reach = rounds[index]
        place = (gx, gy)[axis]
        peers = how_many((place >= reach, place < size - reach))
        pl.semaphore_wait(round_sem.at[index], peers)

    row_y = iota((cells_y, depth), 0)
    col_z = iota((cells_y, depth), 1)

    def y_up(v):
        return jnp.where(row_y == cells_y - 1, 0.0, pltpu.roll(v, cells_y - 1, 0))

    def z_up(v):
        return jnp.where(col_z == depth - 1, 0.0, pltpu.roll(v, depth - 1, 1))

    def y_down(v):
        return jnp.where(row_y == 0, 0.0, pltpu.roll(v, 1, 0))

    def z_down(v):
        return jnp.where(col_z == 0, 0.0, pltpu.roll(v, 1, 1))

    def h_plane(step, x, last):
        elec_now = elec[step]
        ex, ey, ez = elec_now[0, x], elec_now[1, x], elec_now[2, x]
        dx_ey = -ey if last else elec_now[1, x + 1] - ey
        dx_ez = -ez if last else elec_now[2, x + 1] - ez
        magn[0, x] = magn[0, x] - COURANT * ((y_up(ez) - ez) - (z_up(ey) - ey))
        magn[1, x] = magn[1, x] - COURANT * ((z_up(ex) - ex) - dx_ez)
        magn[2, x] = magn[2, x] - COURANT * (dx_ey - (y_up(ex) - ex))

    def e_plane(step, x, first):
        elec_now, elec_new = elec[step], elec[step + 1]
        hx, hy, hz = magn[0, x], magn[1, x], magn[2, x]
        dx_hy = hy if first else hy - magn[1, x - 1]
        dx_hz = hz if first else hz - magn[2, x - 1]
        factor = scale[x]
        elec_new[0, x] = elec_now[0, x] + factor * ((hz - y_down(hz)) - (hy - z_down(hy)))
        elec_new[1, x] = elec_now[1, x] + factor * ((hx - z_down(hx)) - dx_hz)
        elec_new[2, x] = elec_now[2, x] + factor * (dx_hy - (hx - y_down(hx)))

    def loop(low, high, body):
        def run(x, carry):
            body(x)
            return carry

        lax.fori_loop(low, high, run, 0, unroll=True)

    def h_interior(step):
        loop(0, cells_x - 1, lambda x: h_plane(step, x, False))

    def e_interior(step):
        e_plane(step, 0, True)
        loop(1, cells_x, lambda x: e_plane(step, x, False))

    def copy(kind, step, source, target, there, back, dx, dy):
        one = pltpu.make_async_remote_copy(
            src_ref=source,
            dst_ref=target,
            send_sem=send_sem.at[kind, step],
            recv_sem=recv_sem.at[kind, step],
            device_id=(gx + dx, gy + dy),
            device_id_type=MESH,
        )
        return there, back, one

    end_x, end_y = cells_x - 1, cells_y - 1
    top, bottom = pl.ds(0, 1), pl.ds(end_y, 1)
    sent = []
    gate_x, gate_y = first_x.astype(F32), first_y.astype(F32)

    def start(kind, step, *rest):
        there, _, one = copy(kind, step, *rest)
        sent.append((there, one))

        @pl.when(there)
        def _():
            one.start()

    def plans(step):
        corner = pack_corner.at[step]
        return {
            0: (corner.at[0], halo_corner.at[step, 0], last_x & first_y, first_x & last_y, 1, -1),
            1: (corner.at[1], halo_corner.at[step, 1], first_x & last_y, last_x & first_y, -1, 1),
            2: (elec[step].at[pl.ds(1, 2), 0], halo_ex.at[step], first_x, last_x, -1, 0),
            3: (pack_hx.at[step], halo_hx.at[step], last_x, first_x, 1, 0),
            4: (pack_ey.at[step], halo_ey.at[step], first_y, last_y, 0, -1),
            5: (pack_hy.at[step], halo_hy.at[step], last_y, first_y, 0, 1),
        }

    def begin(step, kind):
        start(kind, step, *plans(step)[kind])

    def arrive(step, kind):
        _, back, one = copy(kind, step, *plans(step)[kind])

        @pl.when(back)
        def _():
            one.wait_recv()

    def send_elec_x(step):
        pack_corner[step, 0] = elec[step][0, end_x, top, :]
        pack_corner[step, 1] = elec[step][1, 0, bottom, :]
        begin(step, 0)
        begin(step, 1)
        begin(step, 2)

    def send_elec_y(step):
        pack_ey[step, 0] = elec[step][0, :, top, :]
        pack_ey[step, 1] = elec[step][2, :, top, :]
        begin(step, 4)

    def send_magn_x(step):
        h_plane(step, end_x, True)
        pack_hx[step, 0] = magn[1, end_x]
        pack_hx[step, 1] = magn[2, end_x]
        begin(step, 3)

    def send_magn_y(step):
        pack_hy[step, 0] = magn[0, :, bottom, :]
        pack_hy[step, 1] = magn[2, :, bottom, :]
        begin(step, 5)

    def receive(step):
        now, new = elec[step], elec[step + 1]
        col = iota((cells_x, 1, depth), 2)

        def grow(where, changes):
            terms = []
            for comp, change in changes:
                new[(comp, *where)] = new[(comp, *where)] + change
                if step == STEPS - 1:
                    terms.append(change * weights[(step, comp, *where)])
            for block in range(depth // 128 if terms else 0):
                lanes = sum(term[..., block * 128 : (block + 1) * 128] for term in terms)
                sens[(block, *where)] = sens[(block, *where)] + lanes

        arrive(step, 4)
        arrive(step, 5)
        low, high = (slice(None), top), (slice(None), bottom)
        d_hz = COURANT * halo_ey[step, 0]
        d_hx = -COURANT * halo_ey[step, 1]
        magn[(0, *high)] = magn[(0, *high)] + d_hx
        magn[(2, *high)] = magn[(2, *high)] + d_hz
        before = jnp.concatenate([jnp.zeros_like(d_hz[:1]), d_hz[:-1]], axis=0)
        z_before = jnp.where(col == 0, 0.0, pltpu.roll(d_hx, 1, 2))
        factor = scale[high]
        grow(
            high,
            (
                (0, factor * d_hz),
                (1, factor * ((d_hx - z_before) - (d_hz - before))),
                (2, -factor * d_hx),
            ),
        )
        hx = gate_y * (halo_hy[step, 0] - COURANT * now[(2, *low)])
        hz = gate_y * (halo_hy[step, 1] + COURANT * now[(0, *low)])
        factor = scale[low]
        grow(low, ((0, -factor * hz), (2, factor * hx)))

        for kind in range(4):
            arrive(step, kind)
        corner = COURANT * halo_corner[step]
        hy = gate_x * (halo_hx[step, 0] + COURANT * now[2, 0])
        hz = gate_x * (halo_hx[step, 1] - COURANT * now[1, 0])
        hz = hz + jnp.where(row_y == end_y, corner[0], 0.0)
        factor = scale[0]
        grow((0,), ((1, factor * hz), (2, -factor * hy)))
        d_hy = COURANT * halo_ex[step, 1]
        d_hz = -COURANT * halo_ex[step, 0]
        magn[1, end_x] = magn[1, end_x] + d_hy
        magn[2, end_x] = magn[2, end_x] + d_hz
        y_before = jnp.where(row_y == 0, -corner[1], pltpu.roll(d_hz, 1, 0))
        factor = scale[end_x]
        grow(
            (end_x,),
            (
                (0, factor * ((d_hz - y_before) - (d_hy - z_down(d_hy)))),
                (1, -factor * d_hz),
                (2, factor * d_hy),
            ),
        )

    def clear_missing():
        for missing, buffer in (
            (gx == size_x - 1, halo_ex),
            (gx == 0, halo_hx),
            (gy == size_y - 1, halo_ey),
            (gy == 0, halo_hy),
            ((gx == 0) | (gy == size_y - 1), halo_corner.at[:, 0]),
            ((gx == size_x - 1) | (gy == 0), halo_corner.at[:, 1]),
        ):

            @pl.when(missing)
            def _():
                buffer[...] = jnp.zeros(buffer.shape, F32)

    def wait_sent():
        for there, one in sent:

            @pl.when(there)
            def _():
                one.wait_send()

    def make_scale():
        def plane(x):
            kind = mat[x]
            eps = jnp.full(kind.shape, eps_ref[0], F32)
            for index in range(1, eps_ref.shape[0]):
                eps = jnp.where(kind == index, eps_ref[index], eps)
            scale[x] = COURANT / eps

        loop(0, cells_x, plane)

    def make_coefs():
        width = 2 * waves * cells_y
        column = iota((8, width), 1)
        wave = column // (2 * cells_y)
        phase = jnp.full((8, width), phase_ref[0], F32)
        for index in range(1, waves):
            phase = jnp.where(wave == index, phase_ref[index], phase)
        angle = phase * (iota((8, width), 0) + 1).astype(F32)
        imaginary = lax.rem(column // cells_y, 2) == 1
        values = jnp.where(imaginary, -jnp.sin(angle), jnp.cos(angle)) / float(waves * STEPS)
        own = iota((cells_y, width), 0) == lax.rem(iota((cells_y, width), 1), cells_y)
        table = jnp.concatenate(
            [jnp.where(own, values[step : step + 1], 0.0) for step in range(STEPS)], axis=0
        )
        coefs[...] = jnp.concatenate(split2(table), axis=0)

    def make_weights(low, high):
        half = STEPS * cells_y

        def plane(index):
            comp, x = lax.rem(index, 3), index // 3
            block = dft[:, :, comp, x].reshape(2 * waves * cells_y, depth)
            both = dot(coefs[...], block)
            weights[:, comp, x] = (both[:half] + both[half:]).reshape(STEPS, cells_y, depth)

        def several(index):
            for extra in range(UNROLL):
                plane(index * UNROLL + extra)

        loop(low, high, several)

    def add_sens(low, high):
        def plane(x):
            total = None
            for step in range(low, high):
                for comp in range(3):
                    term = elec[step + 1][comp, x] * weights[step, comp, x]
                    total = term if total is None else total + term
            for block in range(depth // 128):
                lanes = total[:, block * 128 : (block + 1) * 128]
                sens[block, x] = lanes if low == 0 else sens[block, x] + lanes

        loop(0, cells_x, plane)

    def as_column(values):
        pick = (iota((tiles, tile_x), 0) // tile_y == iota((tiles, tile_x), 1)).astype(BF16)
        spread = dot(pick, values.astype(F32).astype(BF16))
        keep = iota((tiles, tile_y), 1) == lax.rem(iota((tiles, tile_y), 0), tile_y)
        return jnp.sum(jnp.where(keep, spread, 0.0), axis=1, keepdims=True)

    def positions():
        own_row = as_row(owner[...])
        own_column = as_column(owner[...])
        earlier = (own_column == own_row) & (iota((tiles, tiles), 0) < iota((tiles, tiles), 1))
        rank = jnp.sum(jnp.where(earlier, 1.0, 0.0), axis=0, keepdims=True)
        return own_row, own_column, rank

    def label_slots():
        own_row, _, rank = positions()
        mine = (iota((count, tiles), 0).astype(F32) == own_row).astype(BF16)
        place = (iota((128, tiles), 0).astype(F32) == rank).astype(F32)
        labels = (place * (as_row(slot[...]) + 1.0)).astype(BF16)
        table = (
            lax.dot_general(mine, labels, (((1,), (1,)), ((), ())), preferred_element_type=F32)
            - 1.0
        )
        put[:, pl.ds(capacity, 1), :] = table.reshape(count, 1, 128)
        position = own_row * float(capacity) + rank
        placement[...] = (iota((count * capacity, tiles), 0).astype(F32) == position).astype(BF16)
        kinds[...] = jnp.broadcast_to(as_column(kid[...]), (tiles, voxels))

    def wait_all(buffer, place):
        part = buffer.at[pl.ds(0, count - 1)]
        pltpu.make_async_copy(part, part, a2a_sem.at[place]).wait()

    def make_kernels():
        for index in range(kernels):
            high, low = split2(kern[index])
            kern_high[:, index * voxels : (index + 1) * voxels] = high
            kern_low[:, index * voxels : (index + 1) * voxels] = low

    units = 3 * cells_x // UNROLL

    def share(part):
        make_weights(units * part // (STEPS - 1), units * (part + 1) // (STEPS - 1))

    loads[8].wait()
    loads[9].wait()
    wait_partners()
    for step in range(STEPS):
        send_elec_x(step)
        if step == 0:
            loads[10].wait()
        send_magn_x(step)
        if step == 0:
            loads[0].wait()
        send_elec_y(step)
        if step == 0:
            loads[1].wait()
        h_interior(step)
        send_magn_y(step)
        if step == 0:
            loads[7].start()
            clear_missing()
        if step == 0:
            loads[6].start()
        end_round(2 * step - 1)
        run_round(2 * step)
        if step == 0:
            loads[2].wait()
            make_scale()
            make_coefs()
        e_interior(step)
        if step == 1:
            loads[7].wait()
            for place in (3, 4, 5):
                loads[place].wait()
            label_slots()
        if step == 1:
            loads[6].wait()
            make_kernels()
        if step > 0:
            share(step - 1)
        if step == STEPS - 1:
            add_sens(0, STEPS)
        end_round(2 * step)
        run_round(2 * step + 1)
        receive(step)
    end_round(2 * STEPS - 1)
    for index in range(2 * STEPS, len(rounds)):
        run_round(index)
        end_round(index)

    parts = []
    for a in range(2):
        for b in range(2):
            for block in range(depth // 128):
                lanes = sens[block, pl.ds(a, cells_x // 2, 2), pl.ds(b, cells_y // 2, 2), :]
                parts.append(lanes.reshape(tiles, 128))
    high, low = split2(jnp.concatenate(parts, axis=1))
    big, small = kern_high[...], kern_low[...]
    both = dot(jnp.concatenate([high, low], axis=0), big)
    total = both[:tiles] + (both[tiles:] + dot(high, small))
    restricted = jnp.zeros((tiles, voxels), F32)
    for index in range(kernels):
        restricted = restricted + jnp.where(
            kinds[...] == float(index), total[:, index * voxels : (index + 1) * voxels], 0.0
        )
    high, low = split2(restricted)
    both = dot(placement[...], jnp.concatenate([high, low], axis=1))
    put[:, pl.ds(0, capacity), :] = (both[:, :voxels] + both[:, voxels:]).reshape(
        count, capacity, voxels
    )
    got[me] = put[me]

    def push(step, carry):
        peer = lax.rem(me + step, count)
        pltpu.make_async_remote_copy(
            src_ref=put.at[peer],
            dst_ref=got.at[me],
            send_sem=a2a_sem.at[0],
            recv_sem=a2a_sem.at[1],
            device_id=(peer // size_y, lax.rem(peer, size_y)),
            device_id_type=MESH,
        ).start()
        return carry

    lax.fori_loop(1, count, push, 0, unroll=True)
    wait_sent()
    wait_all(got, 1)
    wait_all(put, 0)


def finish(capacity, elec, magn, got, e_out, h_out, grad_ref, sems):
    stores = [
        pltpu.make_async_copy(elec, e_out, sems.at[0]),
        pltpu.make_async_copy(magn, h_out, sems.at[1]),
    ]
    for store in stores:
        store.start()
    count, _, voxels = got.shape
    received = got[:, pl.ds(capacity, 1), :].reshape(count, 128)[:, :capacity]
    gather = (
        iota((SLOTS, count * capacity), 0).astype(F32) == as_row(received)
    ).astype(BF16)
    high, low = split2(got[:, pl.ds(0, capacity), :].reshape(count * capacity, voxels))
    grad_ref[...] = dot(gather, high) + dot(gather, low)
    for store in stores:
        store.wait()


def per_device(
    size_x,
    size_y,
    e_field,
    h_field,
    material,
    eps_table,
    forward_dft,
    phase_step,
    interp_kernels,
    kernel_id,
    owner_map,
    slot_map,
):
    count = size_x * size_y
    cells_x, cells_y, depth = material.shape
    kernels, tile_cells, voxels = interp_kernels.shape
    tiles = cells_x * cells_y // 4
    capacity = max(2, (2 * tiles + count - 1) // count)
    field = jax.ShapeDtypeStruct(e_field.shape, F32)
    anywhere = pl.BlockSpec(memory_space=pltpu.HBM)
    here = pl.BlockSpec(memory_space=pltpu.VMEM)
    state = pl.pallas_call(
        functools.partial(kernel, size_x, size_y, capacity),
        out_shape=(
            pltpu.VMEM(e_field.shape, F32),
            pltpu.VMEM(h_field.shape, F32),
            pltpu.VMEM((count, capacity + 1, voxels), F32),
        ),
        in_specs=[pl.BlockSpec(memory_space=pltpu.SMEM)] * 2 + [anywhere] * 8,
        out_specs=(here,) * 3,
        scratch_shapes=[
            pltpu.VMEM((STEPS,) + e_field.shape, F32),
            pltpu.VMEM(material.shape, jnp.int32),
            pltpu.VMEM(material.shape, F32),
            pltpu.VMEM(forward_dft.shape, BF16),
            pltpu.VMEM(interp_kernels.shape, F32),
            pltpu.VMEM((tile_cells, kernels * voxels), BF16),
            pltpu.VMEM((tile_cells, kernels * voxels), BF16),
            pltpu.VMEM(kernel_id.shape, jnp.int32),
            pltpu.VMEM(owner_map.shape, jnp.int32),
            pltpu.VMEM(slot_map.shape, jnp.int32),
            pltpu.VMEM((2 * STEPS * cells_y, 2 * forward_dft.shape[0] * cells_y), BF16),
            pltpu.VMEM((STEPS,) + e_field.shape, F32),
            pltpu.VMEM((depth // 128, cells_x, cells_y, 128), F32),
            pltpu.VMEM((STEPS, 2, cells_y, depth), F32),
            pltpu.VMEM((STEPS, 2, cells_y, depth), F32),
            pltpu.VMEM((STEPS, 2, cells_x, 1, depth), F32),
            pltpu.VMEM((STEPS, 2, cells_x, 1, depth), F32),
            pltpu.VMEM((STEPS, 2, cells_y, depth), F32),
            pltpu.VMEM((STEPS, 2, cells_x, 1, depth), F32),
            pltpu.VMEM((STEPS, 2, cells_x, 1, depth), F32),
            pltpu.VMEM((STEPS, 2, 1, depth), F32),
            pltpu.VMEM((STEPS, 2, 1, depth), F32),
            pltpu.VMEM((count, capacity + 1, voxels), F32),
            pltpu.VMEM((count * capacity, tiles), BF16),
            pltpu.VMEM((tiles, voxels), F32),
            pltpu.SemaphoreType.DMA((11,)),
            pltpu.SemaphoreType.DMA((6, STEPS)),
            pltpu.SemaphoreType.DMA((6, STEPS)),
            pltpu.SemaphoreType.REGULAR((32,)),
            pltpu.SemaphoreType.DMA((2,)),
        ],
        compiler_params=pltpu.CompilerParams(
            collective_id=0, has_side_effects=True, vmem_limit_bytes=60 * 2**20
        ),
    )(
        eps_table,
        phase_step,
        e_field,
        h_field,
        material,
        forward_dft,
        interp_kernels,
        kernel_id,
        owner_map,
        slot_map,
    )
    return pl.pallas_call(
        functools.partial(finish, capacity),
        out_shape=(field, field, jax.ShapeDtypeStruct((SLOTS, voxels), F32)),
        in_specs=[here] * 3,
        out_specs=(anywhere, anywhere, here),
        scratch_shapes=[pltpu.SemaphoreType.DMA((2,))],
        compiler_params=pltpu.CompilerParams(
            has_side_effects=True, vmem_limit_bytes=8 * 2**20
        ),
    )(*[pltpu.with_memory_space_constraint(part, pltpu.VMEM) for part in state])


def solution(mesh):
    return jax.shard_map(
        functools.partial(per_device, mesh.shape["gx"], mesh.shape["gy"]),
        mesh=mesh,
        in_specs=(
            P(None, "gx", "gy", None),
            P(None, "gx", "gy", None),
            P("gx", "gy", None),
            P(),
            P(None, None, None, "gx", "gy", None),
            P(),
            P(),
            P("gx", "gy"),
            P("gx", "gy"),
            P("gx", "gy"),
        ),
        out_specs=(P(None, "gx", "gy", None), P(None, "gx", "gy", None), P(("gx", "gy"), None)),
        check_vma=False,
    )
```
